512 devices in a mesh: ctx: 32 (over y, x, core), hg: 16 (over z).
Axes of the slice: x: 4, y: 4, z: 16, core: 2. Of those that a mesh axis runs over, the one named last changes fastest.
Arguments:
- queries: bfloat16 [65536, 2048], P('ctx', 'hg'), may hold values from -17 to 17
- keys: bfloat16 [65536, 2048], P('ctx', 'hg'), may hold values from -10 to 10
- values: bfloat16 [65536, 2048], P('ctx', 'hg'), may hold values from -8 to 8
- cluster_ids: int32 [16, 65536, 1], P('hg', 'ctx'), may hold values from 0 to 511; in each aligned block of 2048 rows (0 to 2047, 2048 to 4095, ..., all dimensions but the last counted through in order) at most 8 rows name the same one
- w_out: bfloat16 [2048, 2048], P(None, 'hg'), may hold values from -0.125 to 0.125
- old_sums: float32 [16, 512, 128], P('hg', 'ctx'), may hold values from -24 to 24
Outputs:
- projected: bfloat16 [65536, 2048], P('ctx', 'hg')
- centroid_sums: float32 [16, 512, 128], P('hg', 'ctx')
The draws below stay inside these ranges and needn't reach their ends.
Inputs may be any that keep to these rules, and one draw needn't show every extreme that they name: `cluster_ids`: for each head, the 2048 tokens of one index of ctx (aligned blocks along the token dimension) name no cluster more than 8 times, a bound that some block reaches.
All inputs are finite; a program needn't handle non-finite values.
Results may differ from the reference program's by a relative error of at most 0.015.
Values may be sent and summed in bfloat16 or wider, within the bound.
No kernel may reach another device: no remote copies, remote signals or barrier semaphores. Data moves between devices by JAX's collectives and lax.ppermute only.
A program may use at most 64 MiB of HBM per device.

```python
import math
import jax
import jax.numpy as jnp
import numpy as np
from jax import lax

H = 16
HD = 128
NCL = 512
TOK_DEV = 2048
D = 2048
TOKENS = 65536
SLOTS = 8
CAP = 256


def draw_keys(key, part):
    result = jnp.clip(jax.random.normal(jax.random.fold_in(key, 11), (TOKENS, H, HD), jnp.float32), -6.0, 6.0)
    return result.reshape(TOKENS, H * HD).astype(jnp.bfloat16)


def draw_queries(key, part):
    result = jnp.clip(jax.random.normal(jax.random.fold_in(key, 13), (TOKENS, H, HD), jnp.float32), -6.0, 6.0)
    return result.reshape(TOKENS, H * HD).astype(jnp.bfloat16)


def steps_of(own_key, extent, split, low, high):
    gain, own = 1.0, jax.random.fold_in(own_key, 6)
    for dim, blocks in split:
        heights = jnp.exp(jax.random.uniform(jax.random.fold_in(own, dim), (blocks,), jnp.float32, low / len(split), high / len(split)))
        gain = gain * jnp.repeat(heights, extent[dim] // blocks).reshape([-1 if axis == dim else 1 for axis in range(len(extent))])
    return gain


def deal_out(stream_key, own, number, rows, number_of, top, bound, lean):
    order = jax.random.permutation(stream_key, number_of)
    crowded, usual = portions_of(number_of, rows * top, bound, lean, True), portions_of(number_of, rows * top, bound, lean, False)
    places = jnp.arange(number_of)

    def named(tallies, turn):
        used = int((tallies > 0).sum())
        fixed = max(1, used // 4)
        passed = fixed + (places - fixed + turn * (used - fixed)) % max(1, number_of - fixed)
        return jnp.zeros((number_of,), jnp.int32).at[order[jnp.where(places < fixed, places, passed)]].set(jnp.asarray(tallies, jnp.int32))

    tallies = jnp.where(number % 4 == 0, named(crowded, number // 4), named(usual, number - number // 4 - 1))
    mixed = jax.random.permutation(jax.random.fold_in(own, 3), number_of)
    giver, sink = mixed[0:number_of // 2 * 2:2], mixed[1:number_of // 2 * 2:2]
    margin = jnp.minimum(tallies[giver] - 1, bound - tallies[sink]) // 2
    margin = jnp.where((giver == order[0]) | (sink == order[0]) | (tallies[sink] == 0), 0, jnp.maximum(margin, 0))
    passed = jax.random.randint(jax.random.fold_in(own, 4), (number_of // 2,), 0, 1 << 20) % (margin + 1)
    tallies = tallies.at[giver].add(-passed).at[sink].add(passed)
    items = jnp.searchsorted(jnp.cumsum(tallies), jnp.arange(rows * top), side="right").astype(jnp.int32)
    table = items.reshape(top, rows).T
    table = table[jax.random.permutation(jax.random.fold_in(own, 1), rows)]
    turn = jax.random.randint(jax.random.fold_in(own, 2), (rows, 1), 0, top)
    return jnp.take_along_axis(table, (jnp.arange(top)[None, :] + turn) % top, axis=1)


def portions_of(count, total, reach, lean, full):
    loads = [(1 << 20) // math.isqrt(standing ** lean) + 1 for standing in range(1, count + 1)]
    largest = reach if full else min(reach, max(-(-total // count), total * loads[0] // sum(loads)))
    least = 1 if total - largest >= count - 1 else 0
    holding, rest = [largest] + [least] * (count - 1), total - largest - least * (count - 1)
    while rest > 0:
        movable = [i for i in range(1, count) if holding[i] < largest] or [i for i in range(1, count) if holding[i] < reach]
        pool, budget = sum([loads[i] for i in movable]), rest
        for i in movable:
            more = min(reach - holding[i], max(1, budget * loads[i] // pool), rest)
            holding[i] = holding[i] + more
            rest = rest - more
    return np.array(holding)


def normal_values(stream_key, dims, deviation, most, cuts=(), held_as=jnp.bfloat16):
    values = deviation * jax.random.normal(stream_key, dims, jnp.float32)
    if cuts:
        values = values * steps_of(stream_key, dims, cuts, -0.22, 0.18)
    return jnp.clip(values, -most, most).astype(held_as)


def setup_inputs(seed: int = 0) -> dict:
    key_of = jax.random.split(jax.random.key(seed), 7)
    queries = draw_queries(jax.random.fold_in(key_of[6], 71), 0)
    keys = draw_keys(jax.random.fold_in(key_of[6], 71), 0)
    values = normal_values(key_of[2], (TOKENS, D), 2.0, 8.0, ((0, 32), (1, 16)))
    cluster_ids_keys = jax.random.split(jax.random.fold_in(key_of[3], 1), H * TOKENS // TOK_DEV)
    cluster_ids_turns = jax.random.permutation(jax.random.fold_in(key_of[3], 3), H * TOKENS // TOK_DEV)
    cluster_ids = jax.vmap(lambda own, number: deal_out(jax.random.fold_in(key_of[3], 2), own, number, TOK_DEV, NCL, 1, SLOTS, 2))(cluster_ids_keys, cluster_ids_turns).reshape((H, TOKENS, 1))
    w_out = normal_values(key_of[4], (D, D), D ** -0.5, 0.125, ((1, 16),))
    old_sums = normal_values(key_of[5], (H, NCL, HD), 4.0, 24.0, ((0, 16), (1, 32)), jnp.float32)
    return {"queries": queries, "keys": keys, "values": values, "cluster_ids": cluster_ids, "w_out": w_out, "old_sums": old_sums}


DECAY = 0.9
NEG_FILL = -1e30


def one_head(operands):
    query_rows, key_rows, value_rows, cluster_of = operands
    ordering = jnp.argsort(cluster_of, stable=True).astype(jnp.int32)
    sorted_ids = cluster_of[ordering]
    first_slot = jnp.searchsorted(sorted_ids, jnp.arange(NCL, dtype=jnp.int32), side="left").astype(jnp.int32)
    rank_sorted = jnp.arange(TOKENS, dtype=jnp.int32) - first_slot[sorted_ids]
    slot_rank = jnp.zeros((TOKENS,), jnp.int32).at[ordering].set(rank_sorted)
    target = cluster_of * CAP + slot_rank

    def spread(source):
        return jnp.zeros((NCL * CAP, HD), source.dtype).at[target].set(source).reshape(NCL, CAP, HD)

    live_slots = jnp.zeros((NCL * CAP,), jnp.float32).at[target].set(1.0).reshape(NCL, CAP)
    query_slab = spread(query_rows).astype(jnp.float32)
    key_slab = spread(key_rows).astype(jnp.float32)
    value_slab = spread(value_rows).astype(jnp.float32)
    scores = jnp.einsum("cqd,ckd->cqk", query_slab, key_slab) * (HD ** -0.5)
    scores = jnp.where(live_slots[:, None, :] > 0, scores, NEG_FILL)
    row_max = jnp.max(scores, axis=2, keepdims=True)
    weights = jnp.exp(scores - row_max)
    probabilities = (weights / jnp.sum(weights, axis=2, keepdims=True)).astype(jnp.bfloat16)
    mixed_slab = jnp.einsum("cqk,ckd->cqd", probabilities.astype(jnp.float32), value_slab).astype(jnp.bfloat16)
    attention = mixed_slab.reshape(NCL * CAP, HD)[target]
    member_sums = jnp.zeros((NCL, HD), jnp.float32).at[cluster_of].add(key_rows.astype(jnp.float32))
    return attention, member_sums


def reference(queries, keys, values, cluster_ids, w_out, old_sums):
    def by_head(source):
        return source.reshape(TOKENS, H, HD).transpose(1, 0, 2)

    attention, member_sums = lax.map(one_head, (by_head(queries), by_head(keys), by_head(values), cluster_ids[:, :, 0]))
    attention = attention.transpose(1, 0, 2).reshape(TOKENS, D)
    projected = jnp.dot(attention, w_out, preferred_element_type=jnp.float32).astype(jnp.bfloat16)
    centroid_sums = DECAY * old_sums + (1.0 - DECAY) * member_sums
    return (projected, centroid_sums)
```

```python
import jax
import jax.numpy as jnp
from jax import lax
from jax.sharding import PartitionSpec as P

HD = 128
NCL = 512
SLOTS = 8


DECAY = 0.9
NEG_FILL = -1e30


def on_device(queries, keys, values, cluster_ids, w_out, old_sums):
    ctx_count = lax.axis_size("ctx")
    hg_count = lax.axis_size("hg")
    local_count = NCL // ctx_count
    heads_dev = cluster_ids.shape[0]
    tok_rows = queries.shape[0]
    cluster_of = cluster_ids[:, :, 0]
    w_all = lax.all_gather(w_out, "hg", axis=0, tiled=False)

    def split_heads(source):
        return source.reshape(tok_rows, heads_dev, HD).transpose(1, 0, 2)

    packed = jnp.concatenate([split_heads(queries), split_heads(keys), split_heads(values)], axis=2)
    position = jnp.arange(tok_rows, dtype=jnp.int32)

    def rank_one(head_ids):
        same_before = (head_ids[:, None] == head_ids[None, :]) & (
            position[None, :] < position[:, None]
        )
        return jnp.sum(same_before, axis=1, dtype=jnp.int32)

    slot_rank = lax.map(rank_one, cluster_of)
    target = cluster_of * SLOTS + slot_rank

    def place_rows(source, where_to):
        return jnp.zeros((NCL * SLOTS, source.shape[1]), source.dtype).at[where_to].set(source)

    outgoing = jax.vmap(place_rows)(packed, target).reshape(
        heads_dev, ctx_count, local_count, SLOTS, 3 * HD
    )
    live_flags = jax.vmap(place_rows)(jnp.ones((heads_dev, tok_rows, 1), jnp.bfloat16), target)
    live_flags = live_flags.reshape(heads_dev, ctx_count, local_count, SLOTS, 1)
    slab_rows = lax.all_to_all(outgoing, "ctx", split_axis=1, concat_axis=1, tiled=True)
    mark_rows = lax.all_to_all(live_flags, "ctx", split_axis=1, concat_axis=1, tiled=True)
    groups = slab_rows.shape[2]
    key_count = ctx_count * SLOTS
    slab_rows = slab_rows.transpose(0, 2, 1, 3, 4).reshape(heads_dev, groups, key_count, 3 * HD)
    mark_rows = mark_rows.transpose(0, 2, 1, 3, 4).reshape(heads_dev, groups, key_count)
    query_rows = slab_rows[..., :HD]
    key_rows = slab_rows[..., HD : 2 * HD]
    value_rows = slab_rows[..., 2 * HD :]
    scores = jnp.einsum(
        "hcqd,hckd->hcqk", query_rows, key_rows, preferred_element_type=jnp.float32
    ) * HD ** (-0.5)
    present = (mark_rows > 0)[:, :, None, :]
    scores = jnp.where(present, scores, NEG_FILL)
    row_max = jnp.max(scores, axis=3, keepdims=True)
    weights = jnp.exp(scores - row_max)
    probabilities = (weights / jnp.sum(weights, axis=3, keepdims=True)).astype(jnp.bfloat16)
    mixed_rows = jnp.einsum(
        "hcqk,hckd->hcqd", probabilities, value_rows, preferred_element_type=jnp.float32
    ).astype(jnp.bfloat16)
    mixed_rows = mixed_rows.reshape(heads_dev, groups, ctx_count, SLOTS, HD).transpose(
        0, 2, 1, 3, 4
    )
    returned = lax.all_to_all(mixed_rows, "ctx", split_axis=1, concat_axis=1, tiled=True)
    flat_back = returned.reshape(heads_dev, NCL * SLOTS, HD)
    attention = jnp.take_along_axis(flat_back, target[:, :, None], axis=1)
    attention = attention.reshape(heads_dev, hg_count, tok_rows // hg_count, HD)
    all_heads = lax.all_to_all(attention, "hg", split_axis=1, concat_axis=1, tiled=True)
    all_heads = all_heads.reshape(hg_count, tok_rows // hg_count, HD)
    w_all = w_all.reshape(hg_count, hg_count, HD, w_out.shape[1])
    mixed = jnp.einsum(
        "htd,nhdf->ntf", all_heads, w_all, preferred_element_type=jnp.float32
    ).astype(jnp.bfloat16)
    projected = lax.all_to_all(mixed, "hg", split_axis=0, concat_axis=0, tiled=True)
    projected = projected.reshape(tok_rows, w_out.shape[1])
    member_sums = jnp.sum(key_rows.astype(jnp.float32), axis=2)
    centroid_sums = DECAY * old_sums + (1.0 - DECAY) * member_sums
    return (projected, centroid_sums)


def solution(mesh):
    placed = (
        P("ctx", "hg"),
        P("ctx", "hg"),
        P("ctx", "hg"),
        P("hg", "ctx", None),
        P(None, "hg"),
        P("hg", "ctx", None),
    )
    return jax.shard_map(
        on_device,
        mesh=mesh,
        in_specs=placed,
        out_specs=(P("ctx", "hg"), P("hg", "ctx", None)),
        check_vma=False,
    )
```

```python
import jax
import jax.numpy as jnp
from jax import lax
from jax.experimental import pallas as pl
from jax.experimental.pallas import tpu as pltpu
from jax.sharding import PartitionSpec as P

HD = 128
NCL = 512
SLOTS = 8
CTX = 32
LOCAL = NCL // CTX
PAIR = LOCAL * SLOTS
TILE = 128

DECAY = 0.9
NEG_FILL = -1e30
EMPTY = 1024.0

F32 = jnp.float32
BF16 = jnp.bfloat16


def place_kernel(ids_ref, q_ref, k_ref, v_ref, out_ref, target_ref, rows, slot_hot, dest_row):
    step = pl.program_id(0)
    per_step = out_ref.shape[0]
    tokens = ids_ref.shape[1]

    @pl.when(step == 0)
    def _():
        ids = ids_ref[...]
        wide = ids.astype(F32)
        before = lax.broadcasted_iota(jnp.int32, (TILE, TILE), 0) < lax.broadcasted_iota(
            jnp.int32, (TILE, TILE), 1
        )
        columns = [wide[:, i * TILE : (i + 1) * TILE] for i in range(tokens // TILE)]
        down = [jnp.transpose(jnp.broadcast_to(c, (TILE, TILE))) for c in columns]
        ranks = []
        for j, column in enumerate(columns):
            here = jnp.broadcast_to(column, (TILE, TILE))
            same = jnp.where((down[j] == here) & before, 1.0, 0.0)
            for i in range(j):
                same = same + jnp.where(down[i] == here, 1.0, 0.0)
            ranks.append(jnp.sum(same, axis=0, keepdims=True))
        rank = jnp.concatenate(ranks, axis=1).astype(jnp.int32)
        target_ref[...] = ids * SLOTS + rank
        slot = (ids % LOCAL) * SLOTS + rank
        slots = lax.broadcasted_iota(jnp.int32, (PAIR, tokens), 0)
        slot_hot[...] = jnp.where(slots == slot, 1.0, 0.0).astype(BF16)
        dest_row[...] = ids // LOCAL
        rows[:, 0:HD] = q_ref[...]
        rows[:, HD : 2 * HD] = k_ref[...]
        rows[:, 2 * HD : 3 * HD] = v_ref[...]
        rows[:, 3 * HD : 4 * HD] = jnp.ones((tokens, HD), BF16)

    first_lane = lax.broadcasted_iota(jnp.int32, (PAIR, HD), 1) == 0
    for i in range(per_step):
        mine = jnp.where(dest_row[...] == step * per_step + i, 1.0, 0.0)
        mine = jnp.broadcast_to(mine, (16, tokens)).astype(BF16)
        hot = slot_hot[...].reshape(PAIR // 16, 16, tokens) * mine[None]
        placed = jnp.dot(hot.reshape(PAIR, tokens), rows[...], preferred_element_type=F32)
        filled = placed[:, 3 * HD : 4 * HD]
        mark = jnp.where(first_lane, EMPTY * (1.0 - filled), 0.0)
        out_ref[i, 0] = placed[:, 0:HD].astype(BF16)
        out_ref[i, 1] = (placed[:, HD : 2 * HD] + mark).astype(BF16)
        out_ref[i, 2] = placed[:, 2 * HD : 3 * HD].astype(BF16)


def place(ids_row, queries, keys, values, per_step=2):
    tokens = queries.shape[0]
    whole = pl.BlockSpec((tokens, HD), lambda s: (0, 0))
    line = pl.BlockSpec((1, tokens), lambda s: (0, 0))
    return pl.pallas_call(
        place_kernel,
        grid=(CTX // per_step,),
        out_shape=(
            jax.ShapeDtypeStruct((CTX, 3, PAIR, HD), BF16),
            jax.ShapeDtypeStruct((1, tokens), jnp.int32),
        ),
        in_specs=[line, whole, whole, whole],
        out_specs=(pl.BlockSpec((per_step, 3, PAIR, HD), lambda s: (s, 0, 0, 0)), line),
        scratch_shapes=[
            pltpu.VMEM((tokens, 4 * HD), BF16),
            pltpu.VMEM((PAIR, tokens), BF16),
            pltpu.VMEM((1, tokens), jnp.int32),
        ],
        compiler_params=pltpu.CompilerParams(
            dimension_semantics=("arbitrary",), vmem_limit_bytes=32 << 20
        ),
        cost_estimate=pl.CostEstimate(
            flops=2 * NCL * SLOTS * tokens * 4 * HD, bytes_accessed=5 << 20, transcendentals=0
        ),
        name="place",
    )(ids_row, queries, keys, values)


def attend_kernel(q_ref, k_ref, v_ref, old_ref, out_ref, sums_ref):
    step = pl.program_id(0)
    sources = q_ref.shape[0]
    members = sources * SLOTS

    def halves(ref):
        both = ref[...].reshape(sources, 2 * SLOTS, HD).astype(F32)
        return [
            both[:, i * SLOTS : (i + 1) * SLOTS].reshape(members, HD).astype(BF16)
            for i in range(2)
        ]

    first_lane = (lax.broadcasted_iota(jnp.int32, (16, HD), 1) == 0).astype(BF16)
    dims = (((1,), (1,)), ((), ()))
    mixed, sums = [], []
    for q, k, v in zip(halves(q_ref), halves(k_ref), halves(v_ref)):
        marks = lax.dot_general(first_lane, k, dims, preferred_element_type=F32)
        present = marks < 0.5 * EMPTY
        scores = lax.dot_general(q, k, dims, preferred_element_type=F32) * HD ** (-0.5)
        scores = jnp.where(present[0:1], scores, NEG_FILL)
        weights = jnp.exp(scores - jnp.max(scores, axis=1, keepdims=True))
        share = weights / jnp.sum(weights, axis=1, keepdims=True)
        mixed.append(
            jnp.dot(share.astype(BF16), v, preferred_element_type=F32).reshape(sources, SLOTS, HD)
        )
        live = jnp.where(present, 1.0, 0.0).astype(BF16)
        sums.append(jnp.dot(live, k, preferred_element_type=F32)[0:1])
    out_ref[...] = jnp.concatenate(mixed, axis=1).astype(BF16)
    member_sums = jnp.concatenate(sums, axis=0)
    two = pl.ds(2 * step, 2)
    sums_ref[two, :] = DECAY * old_ref[two, :] + (1.0 - DECAY) * member_sums


def attend(slab, old_sums):
    def part(which):
        return pl.BlockSpec((CTX, 1, 2 * SLOTS, HD), lambda s: (0, which, s, 0))

    cell = pl.BlockSpec((LOCAL, HD), lambda s: (0, 0))
    return pl.pallas_call(
        attend_kernel,
        grid=(LOCAL // 2,),
        out_shape=(
            jax.ShapeDtypeStruct((CTX, PAIR, HD), BF16),
            jax.ShapeDtypeStruct((LOCAL, HD), F32),
        ),
        in_specs=[part(0), part(1), part(2), cell],
        out_specs=(pl.BlockSpec((CTX, 2 * SLOTS, HD), lambda s: (0, s, 0)), cell),
        compiler_params=pltpu.CompilerParams(
            dimension_semantics=("arbitrary",), vmem_limit_bytes=32 << 20
        ),
        cost_estimate=pl.CostEstimate(
            flops=4 * LOCAL * 256 * 256 * HD,
            bytes_accessed=5 << 20,
            transcendentals=LOCAL * 256 * 256,
        ),
        name="attend",
    )(slab, slab, slab, old_sums)


def on_device(queries, keys, values, cluster_ids, w_out, old_sums):
    hg_count = lax.axis_size("hg")
    tok_rows = queries.shape[0]
    w_all = lax.all_gather(w_out, "hg", axis=0, tiled=False)
    outgoing, target = place(cluster_ids[:, :, 0], queries, keys, values)
    slab = lax.all_to_all(outgoing, "ctx", split_axis=0, concat_axis=0, tiled=True)
    mixed_rows, centroid_sums = attend(slab, old_sums[0])
    returned = lax.all_to_all(mixed_rows, "ctx", split_axis=0, concat_axis=0, tiled=True)
    flat_back = returned.reshape(NCL * SLOTS, HD)
    attention = jnp.take(flat_back, target[0], axis=0, mode="clip")
    attention = attention.reshape(hg_count, tok_rows // hg_count, HD)
    all_heads = lax.all_to_all(attention, "hg", split_axis=0, concat_axis=0, tiled=True)
    w_all = w_all.reshape(hg_count, hg_count, HD, w_out.shape[1])
    mixed = jnp.einsum("htd,nhdf->ntf", all_heads, w_all, preferred_element_type=F32).astype(BF16)
    projected = lax.all_to_all(mixed, "hg", split_axis=0, concat_axis=0, tiled=True)
    return (projected.reshape(tok_rows, w_out.shape[1]), centroid_sums[None])


def solution(mesh):
    placed = (
        P("ctx", "hg"),
        P("ctx", "hg"),
        P("ctx", "hg"),
        P("hg", "ctx", None),
        P(None, "hg"),
        P("hg", "ctx", None),
    )
    return jax.shard_map(
        on_device,
        mesh=mesh,
        in_specs=placed,
        out_specs=(P("ctx", "hg"), P("hg", "ctx", None)),
        check_vma=False,
    )
```

```python
import jax
import jax.numpy as jnp
from jax import lax
from jax.experimental import pallas as pl
from jax.experimental.pallas import tpu as pltpu
from jax.sharding import PartitionSpec as P

HD = 128
NCL = 512
SLOTS = 8
CTX = 32
LOCAL = NCL // CTX
PAIR = LOCAL * SLOTS
TILE = 128

DECAY = 0.9
NEG_FILL = -1e30
EMPTY = 1024.0

EXP2_SCALE = HD ** (-0.5) * 1.4426950408889634

F32 = jnp.float32
BF16 = jnp.bfloat16


def place_kernel(
    core_ref, ids_ref, q_ref, k_ref, v_ref, w_ref, out_ref, target_ref, half_ref, rows, slot_hot, hot, dest_row
):
    del core_ref
    step = pl.program_id(0)
    per_step = out_ref.shape[0]
    tokens = ids_ref.shape[1]

    @pl.when(step == 0)
    def _():
        ids = ids_ref[...]
        wide = ids.astype(F32)
        before = lax.broadcasted_iota(jnp.int32, (TILE, TILE), 0) < lax.broadcasted_iota(
            jnp.int32, (TILE, TILE), 1
        )
        columns = [wide[:, i * TILE : (i + 1) * TILE] for i in range(tokens // TILE)]
        down = [jnp.transpose(jnp.broadcast_to(c, (TILE, TILE))) for c in columns]
        ranks = []
        for j, column in enumerate(columns):
            here = jnp.broadcast_to(column, (TILE, TILE))
            same = jnp.where((down[j] == here) & before, 1.0, 0.0)
            for i in range(j):
                same = same + jnp.where(down[i] == here, 1.0, 0.0)
            ranks.append(jnp.sum(same, axis=0, keepdims=True))
        rank = jnp.concatenate(ranks, axis=1).astype(jnp.int32)
        target_ref[...] = ids * SLOTS + rank
        half_ref[...] = w_ref[...]
        slot = (ids % LOCAL) * SLOTS + rank
        slots = lax.broadcasted_iota(jnp.int32, (PAIR, tokens), 0)
        slot_hot[...] = jnp.where(slots == slot, 1.0, 0.0).astype(BF16)
        dest_row[...] = ids // LOCAL
        rows[:, 0:HD] = k_ref[...]
        rows[:, HD : 2 * HD] = jnp.ones((tokens, HD), BF16)
        rows[:, 2 * HD : 3 * HD] = q_ref[...]
        rows[:, 3 * HD : 4 * HD] = v_ref[...]

    for i in range(per_step):
        mine = jnp.where(dest_row[...] == step * per_step + i, 1.0, 0.0)
        mine = jnp.broadcast_to(mine, (16, tokens)).astype(BF16)
        here = slot_hot[...].reshape(PAIR // 16, 16, tokens) * mine[None]
        hot[i * PAIR : (i + 1) * PAIR, :] = here.reshape(PAIR, tokens)
    shape = (per_step, PAIR, HD)
    keyed = jnp.dot(hot[...], rows[:, 0 : 2 * HD], preferred_element_type=F32)
    filled = keyed[:, HD : 2 * HD]
    first_lane = lax.broadcasted_iota(jnp.int32, filled.shape, 1) == 0
    marked = keyed[:, 0:HD] + jnp.where(first_lane, EMPTY * (1.0 - filled), 0.0)
    out_ref[:, 1] = marked.astype(BF16).reshape(shape)
    others = jnp.dot(hot[...], rows[:, 2 * HD : 4 * HD], preferred_element_type=F32)
    out_ref[:, 0] = others[:, 0:HD].astype(BF16).reshape(shape)
    out_ref[:, 2] = others[:, HD : 2 * HD].astype(BF16).reshape(shape)


def place(core, ids_row, queries, keys, values, w_out, per_step=8):
    tokens = queries.shape[0]
    half = w_out.shape[0] // 2
    whole = pl.BlockSpec((tokens, HD), lambda s, c: (0, 0))
    line = pl.BlockSpec((1, tokens), lambda s, c: (0, 0))
    return pl.pallas_call(
        place_kernel,
        grid_spec=pltpu.PrefetchScalarGridSpec(
            num_scalar_prefetch=1,
            grid=(CTX // per_step,),
            in_specs=[
                line,
                whole,
                whole,
                whole,
                pl.BlockSpec((half, w_out.shape[1]), lambda s, c: (c[0], 0)),
            ],
            out_specs=(
                pl.BlockSpec((per_step, 3, PAIR, HD), lambda s, c: (s, 0, 0, 0)),
                line,
                pl.BlockSpec((half, w_out.shape[1]), lambda s, c: (0, 0)),
            ),
            scratch_shapes=[
                pltpu.VMEM((tokens, 4 * HD), BF16),
                pltpu.VMEM((PAIR, tokens), BF16),
                pltpu.VMEM((per_step * PAIR, tokens), BF16),
                pltpu.VMEM((1, tokens), jnp.int32),
            ],
        ),
        out_shape=(
            jax.ShapeDtypeStruct((CTX, 3, PAIR, HD), BF16),
            jax.ShapeDtypeStruct((1, tokens), jnp.int32),
            jax.ShapeDtypeStruct((half, w_out.shape[1]), BF16),
        ),
        compiler_params=pltpu.CompilerParams(
            dimension_semantics=("arbitrary",), vmem_limit_bytes=60 << 20
        ),
        cost_estimate=pl.CostEstimate(
            flops=2 * NCL * SLOTS * tokens * 4 * HD, bytes_accessed=5 << 20, transcendentals=0
        ),
        name="place",
    )(core, ids_row, queries, keys, values, w_out)


def attend_kernel(q_ref, k_ref, v_ref, old_ref, out_ref, sums_ref):
    step = pl.program_id(0)
    sources, block = q_ref.shape[0], q_ref.shape[2]
    count = block // SLOTS
    members = sources * SLOTS

    def split(ref):
        whole = ref[...].reshape(sources, block, HD).astype(F32)
        return [
            whole[:, i * SLOTS : (i + 1) * SLOTS].reshape(members, HD).astype(BF16)
            for i in range(count)
        ]

    first_lane = (lax.broadcasted_iota(jnp.int32, (16, HD), 1) == 0).astype(BF16)
    ones = jnp.ones((members, HD), BF16)
    dims = (((1,), (1,)), ((), ()))
    mixed, sums = [], []
    for q, k, v in zip(split(q_ref), split(k_ref), split(v_ref)):
        marks = lax.dot_general(first_lane, k, dims, preferred_element_type=F32)
        present = marks < 0.5 * EMPTY
        scores = lax.dot_general(q, k, dims, preferred_element_type=F32)
        scores = jnp.where(present[0:1], scores, NEG_FILL)
        weights = jnp.exp2((scores - jnp.max(scores, axis=1, keepdims=True)) * EXP2_SCALE)
        totals = jnp.dot(
            weights.astype(BF16), jnp.concatenate([v, ones], axis=1), preferred_element_type=F32
        )
        mixed.append((totals[:, 0:HD] / totals[:, HD:]).reshape(sources, SLOTS, HD))
        live = jnp.where(present, 1.0, 0.0).astype(BF16)
        sums.append(jnp.dot(live, k, preferred_element_type=F32)[0:1])
    out_ref[...] = jnp.concatenate(mixed, axis=1).astype(BF16)
    member_sums = jnp.concatenate(sums, axis=0)
    these = pl.ds(count * step, count)
    sums_ref[these, :] = DECAY * old_ref[these, :] + (1.0 - DECAY) * member_sums


def attend(slab, old_sums, count=4):
    def part(which):
        return pl.BlockSpec((CTX, 1, count * SLOTS, HD), lambda s: (0, which, s, 0))

    cell = pl.BlockSpec((LOCAL, HD), lambda s: (0, 0))
    return pl.pallas_call(
        attend_kernel,
        grid=(LOCAL // count,),
        out_shape=(
            jax.ShapeDtypeStruct((CTX, PAIR, HD), BF16),
            jax.ShapeDtypeStruct((LOCAL, HD), F32),
        ),
        in_specs=[part(0), part(1), part(2), cell],
        out_specs=(pl.BlockSpec((CTX, count * SLOTS, HD), lambda s: (0, s, 0)), cell),
        compiler_params=pltpu.CompilerParams(
            dimension_semantics=("arbitrary",), vmem_limit_bytes=32 << 20
        ),
        cost_estimate=pl.CostEstimate(
            flops=4 * LOCAL * 256 * 256 * HD,
            bytes_accessed=5 << 20,
            transcendentals=LOCAL * 256 * 256,
        ),
        name="attend",
    )(slab, slab, slab, old_sums)


def fetch_kernel(target_ref, back_ref, out_ref):
    tokens = out_ref.shape[0]
    lanes = lax.broadcasted_iota(jnp.int32, (TILE, PAIR), 1)
    for j in range(tokens // TILE):
        here = target_ref[:, j * TILE : (j + 1) * TILE].astype(F32)
        down = jnp.transpose(jnp.broadcast_to(here, (TILE, TILE))).astype(jnp.int32)
        dest = down // PAIR
        slot = jnp.where(lanes == down % PAIR, 1.0, 0.0)
        hot = [jnp.where(dest % 8 == i, slot, 0.0).astype(BF16) for i in range(8)]
        found = jnp.dot(
            jnp.concatenate(hot, axis=1),
            jnp.concatenate(
                [back_ref[8 * i : 8 * i + 8].reshape(8 * PAIR, HD) for i in range(CTX // 8)], axis=1
            ),
            preferred_element_type=F32,
        )
        row = found[:, 0:HD]
        for i in range(1, CTX // 8):
            row = jnp.where(dest // 8 == i, found[:, i * HD : (i + 1) * HD], row)
        out_ref[j * TILE : (j + 1) * TILE, :] = row.astype(BF16)


def fetch(target, back, tile=1024):
    tokens = target.shape[1]
    return pl.pallas_call(
        fetch_kernel,
        grid=(tokens // tile,),
        out_shape=jax.ShapeDtypeStruct((tokens, HD), BF16),
        in_specs=[
            pl.BlockSpec((1, tile), lambda s: (0, s)),
            pl.BlockSpec((CTX, PAIR, HD), lambda s: (0, 0, 0)),
        ],
        out_specs=pl.BlockSpec((tile, HD), lambda s: (s, 0)),
        compiler_params=pltpu.CompilerParams(
            dimension_semantics=("arbitrary",), vmem_limit_bytes=32 << 20
        ),
        cost_estimate=pl.CostEstimate(
            flops=2 * tokens * 1024 * 512, bytes_accessed=2 << 20, transcendentals=0
        ),
        name="fetch",
    )(target, back)


def project_kernel(heads_ref, w_ref, out_ref):
    halves, columns = w_ref.shape[0], w_ref.shape[1]
    each = heads_ref.shape[0] // halves
    total = 0.0
    for c in range(halves):
        left = jnp.concatenate([heads_ref[c * each + i] for i in range(each)], axis=1)
        right = jnp.concatenate([w_ref[c, n] for n in range(columns)], axis=1)
        total = total + jnp.dot(left, right, preferred_element_type=F32)
    for n in range(columns):
        out_ref[n] = total[:, n * HD : (n + 1) * HD].astype(BF16)


def project(heads, w_all, columns=2):
    halves, blocks, depth, width = w_all.shape
    tokens = heads.shape[1]
    return pl.pallas_call(
        project_kernel,
        grid=(blocks // columns,),
        out_shape=jax.ShapeDtypeStruct((blocks, tokens, width), BF16),
        in_specs=[
            pl.BlockSpec(heads.shape, lambda s: (0, 0, 0)),
            pl.BlockSpec((halves, columns, depth, width), lambda s: (0, s, 0, 0)),
        ],
        out_specs=pl.BlockSpec((columns, tokens, width), lambda s: (s, 0, 0)),
        compiler_params=pltpu.CompilerParams(
            dimension_semantics=("arbitrary",), vmem_limit_bytes=60 << 20
        ),
        cost_estimate=pl.CostEstimate(
            flops=2 * tokens * halves * depth * blocks * width,
            bytes_accessed=9 << 20,
            transcendentals=0,
        ),
        name="project",
    )(heads, w_all)


def on_device(queries, keys, values, cluster_ids, w_out, old_sums):
    hg_count = lax.axis_size("hg")
    tok_rows = queries.shape[0]
    core = (lax.axis_index("ctx") % 2).astype(jnp.int32).reshape(1)
    outgoing, target, w_half = place(core, cluster_ids[:, :, 0], queries, keys, values, w_out)
    chips = [list(range(2 * hg_count * i, 2 * hg_count * (i + 1))) for i in range(CTX // 2)]
    w_all = lax.all_gather(w_half, ("ctx", "hg"), axis_index_groups=chips)
    slab = lax.all_to_all(outgoing, "ctx", split_axis=0, concat_axis=0, tiled=True)
    mixed_rows, centroid_sums = attend(slab, old_sums[0])
    returned = lax.all_to_all(mixed_rows, "ctx", split_axis=0, concat_axis=0, tiled=True)
    attention = fetch(target, returned).reshape(hg_count, tok_rows // hg_count, HD)
    all_heads = lax.all_to_all(attention, "hg", split_axis=0, concat_axis=0, tiled=True)
    mixed = project(all_heads, w_all.reshape(2, hg_count, -1, w_out.shape[1]))
    projected = lax.all_to_all(mixed, "hg", split_axis=0, concat_axis=0, tiled=True)
    return (projected.reshape(tok_rows, w_out.shape[1]), centroid_sums[None])


def solution(mesh):
    placed = (
        P("ctx", "hg"),
        P("ctx", "hg"),
        P("ctx", "hg"),
        P("hg", "ctx", None),
        P(None, "hg"),
        P("hg", "ctx", None),
    )
    return jax.shard_map(
        on_device,
        mesh=mesh,
        in_specs=placed,
        out_specs=(P("ctx", "hg"), P("hg", "ctx", None)),
        check_vma=False,
    )
```

```python
import functools

import jax
import jax.numpy as jnp
from jax import lax
from jax.experimental import pallas as pl
from jax.experimental.pallas import tpu as pltpu
from jax.sharding import PartitionSpec as P

HD = 128
NCL = 512
SLOTS = 8
CTX = 32
LOCAL = NCL // CTX
PAIR = LOCAL * SLOTS
ROOM = 96
META = 8
CHUNK = 3 * ROOM + META
NO_ROW = 255.0
TILE = 128

DECAY = 0.9
NEG_FILL = -1e30
EMPTY = 1024.0

EXP2_SCALE = HD ** (-0.5) * 1.4426950408889634

F32 = jnp.float32
BF16 = jnp.bfloat16


def ranks_of(ids):
    wide = ids.astype(F32)
    before = lax.broadcasted_iota(jnp.int32, (TILE, TILE), 0) < lax.broadcasted_iota(
        jnp.int32, (TILE, TILE), 1
    )
    columns = [wide[:, i * TILE : (i + 1) * TILE] for i in range(ids.shape[1] // TILE)]
    down = [jnp.transpose(jnp.broadcast_to(c, (TILE, TILE))) for c in columns]
    ranks = []
    for j, column in enumerate(columns):
        here = jnp.broadcast_to(column, (TILE, TILE))
        same = jnp.where((down[j] == here) & before, 1.0, 0.0)
        for i in range(j):
            same = same + jnp.where(down[i] == here, 1.0, 0.0)
        ranks.append(jnp.sum(same, axis=0, keepdims=True))
    return jnp.concatenate(ranks, axis=1).astype(jnp.int32), down


def place_kernel(
    ids_ref, q_ref, k_ref, v_ref, out_ref, target_ref, rows, slot_hot, hot, dest_row
):
    step = pl.program_id(0)
    per_step = out_ref.shape[0]
    tokens = ids_ref.shape[1]

    @pl.when(step == 0)
    def _():
        ids = ids_ref[...]
        rank, _ = ranks_of(ids)
        target_ref[...] = ids * SLOTS + rank
        slot = (ids % LOCAL) * SLOTS + rank
        slots = lax.broadcasted_iota(jnp.int32, (PAIR, tokens), 0)
        slot_hot[...] = jnp.where(slots == slot, 1.0, 0.0).astype(BF16)
        dest_row[...] = ids // LOCAL
        rows[:, 0:HD] = k_ref[...]
        rows[:, HD : 2 * HD] = jnp.ones((tokens, HD), BF16)
        rows[:, 2 * HD : 3 * HD] = q_ref[...]
        rows[:, 3 * HD : 4 * HD] = v_ref[...]

    for i in range(per_step):
        mine = jnp.where(dest_row[...] == step * per_step + i, 1.0, 0.0)
        mine = jnp.broadcast_to(mine, (16, tokens)).astype(BF16)
        here = slot_hot[...].reshape(PAIR // 16, 16, tokens) * mine[None]
        hot[i * PAIR : (i + 1) * PAIR, :] = here.reshape(PAIR, tokens)
    shape = (per_step, PAIR, HD)
    keyed = jnp.dot(hot[...], rows[:, 0 : 2 * HD], preferred_element_type=F32)
    filled = keyed[:, HD : 2 * HD]
    first_lane = lax.broadcasted_iota(jnp.int32, filled.shape, 1) == 0
    marked = keyed[:, 0:HD] + jnp.where(first_lane, EMPTY * (1.0 - filled), 0.0)
    out_ref[:, 1] = marked.astype(BF16).reshape(shape)
    others = jnp.dot(hot[...], rows[:, 2 * HD : 4 * HD], preferred_element_type=F32)
    out_ref[:, 0] = others[:, 0:HD].astype(BF16).reshape(shape)
    out_ref[:, 2] = others[:, HD : 2 * HD].astype(BF16).reshape(shape)


def place(ids_row, queries, keys, values, per_step=8):
    tokens = queries.shape[0]
    whole = pl.BlockSpec((tokens, HD), lambda s: (0, 0))
    line = pl.BlockSpec((1, tokens), lambda s: (0, 0))
    return pl.pallas_call(
        place_kernel,
        grid_spec=pltpu.PrefetchScalarGridSpec(
            num_scalar_prefetch=0,
            grid=(CTX // per_step,),
            in_specs=[
                line,
                whole,
                whole,
                whole,
            ],
            out_specs=(
                pl.BlockSpec((per_step, 3, PAIR, HD), lambda s: (s, 0, 0, 0)),
                line,
            ),
            scratch_shapes=[
                pltpu.VMEM((tokens, 4 * HD), BF16),
                pltpu.VMEM((PAIR, tokens), BF16),
                pltpu.VMEM((per_step * PAIR, tokens), BF16),
                pltpu.VMEM((1, tokens), jnp.int32),
            ],
        ),
        out_shape=(
            jax.ShapeDtypeStruct((CTX, 3, PAIR, HD), BF16),
            jax.ShapeDtypeStruct((1, tokens), jnp.int32),
        ),
        compiler_params=pltpu.CompilerParams(
            dimension_semantics=("arbitrary",), vmem_limit_bytes=60 << 20
        ),
        cost_estimate=pl.CostEstimate(
            flops=2 * NCL * SLOTS * tokens * 4 * HD, bytes_accessed=5 << 20, transcendentals=0
        ),
        name="place",
    )(ids_row, queries, keys, values)


def attend_kernel(q_ref, k_ref, v_ref, old_ref, out_ref, sums_ref):
    step = pl.program_id(0)
    sources, block = q_ref.shape[0], q_ref.shape[2]
    count = block // SLOTS
    members = sources * SLOTS

    def split(ref):
        whole = ref[...].reshape(sources, block, HD).astype(F32)
        return [
            whole[:, i * SLOTS : (i + 1) * SLOTS].reshape(members, HD).astype(BF16)
            for i in range(count)
        ]

    first_lane = (lax.broadcasted_iota(jnp.int32, (16, HD), 1) == 0).astype(BF16)
    ones = jnp.ones((members, HD), BF16)
    dims = (((1,), (1,)), ((), ()))
    mixed, sums = [], []
    for q, k, v in zip(split(q_ref), split(k_ref), split(v_ref)):
        marks = lax.dot_general(first_lane, k, dims, preferred_element_type=F32)
        present = marks < 0.5 * EMPTY
        scores = lax.dot_general(q, k, dims, preferred_element_type=F32)
        scores = jnp.where(present[0:1], scores, NEG_FILL)
        weights = jnp.exp2((scores - jnp.max(scores, axis=1, keepdims=True)) * EXP2_SCALE)
        totals = jnp.dot(
            weights.astype(BF16), jnp.concatenate([v, ones], axis=1), preferred_element_type=F32
        )
        mixed.append((totals[:, 0:HD] / totals[:, HD:]).reshape(sources, SLOTS, HD))
        live = jnp.where(present, 1.0, 0.0).astype(BF16)
        sums.append(jnp.dot(live, k, preferred_element_type=F32)[0:1])
    out_ref[...] = jnp.concatenate(mixed, axis=1).astype(BF16)
    member_sums = jnp.concatenate(sums, axis=0)
    these = pl.ds(count * step, count)
    sums_ref[these, :] = DECAY * old_ref[these, :] + (1.0 - DECAY) * member_sums


def attend(slab, old_sums, count=4):
    def part(which):
        return pl.BlockSpec((CTX, 1, count * SLOTS, HD), lambda s: (0, which, s, 0))

    cell = pl.BlockSpec((LOCAL, HD), lambda s: (0, 0))
    return pl.pallas_call(
        attend_kernel,
        grid=(LOCAL // count,),
        out_shape=(
            jax.ShapeDtypeStruct((CTX, PAIR, HD), BF16),
            jax.ShapeDtypeStruct((LOCAL, HD), F32),
        ),
        in_specs=[part(0), part(1), part(2), cell],
        out_specs=(pl.BlockSpec((CTX, count * SLOTS, HD), lambda s: (0, s, 0)), cell),
        compiler_params=pltpu.CompilerParams(
            dimension_semantics=("arbitrary",), vmem_limit_bytes=32 << 20
        ),
        cost_estimate=pl.CostEstimate(
            flops=4 * LOCAL * 256 * 256 * HD,
            bytes_accessed=5 << 20,
            transcendentals=LOCAL * 256 * 256,
        ),
        name="attend",
    )(slab, slab, slab, old_sums)


def fetch_kernel(target_ref, back_ref, out_ref):
    tokens = out_ref.shape[0]
    lanes = lax.broadcasted_iota(jnp.int32, (TILE, PAIR), 1)
    for j in range(tokens // TILE):
        here = target_ref[:, j * TILE : (j + 1) * TILE].astype(F32)
        down = jnp.transpose(jnp.broadcast_to(here, (TILE, TILE))).astype(jnp.int32)
        dest = down // PAIR
        slot = jnp.where(lanes == down % PAIR, 1.0, 0.0)
        hot = [jnp.where(dest % 8 == i, slot, 0.0).astype(BF16) for i in range(8)]
        found = jnp.dot(
            jnp.concatenate(hot, axis=1),
            jnp.concatenate(
                [back_ref[8 * i : 8 * i + 8].reshape(8 * PAIR, HD) for i in range(CTX // 8)], axis=1
            ),
            preferred_element_type=F32,
        )
        row = found[:, 0:HD]
        for i in range(1, CTX // 8):
            row = jnp.where(dest // 8 == i, found[:, i * HD : (i + 1) * HD], row)
        out_ref[j * TILE : (j + 1) * TILE, :] = row.astype(BF16)


def fetch(target, back, tile=1024):
    tokens = target.shape[1]
    return pl.pallas_call(
        fetch_kernel,
        grid=(tokens // tile,),
        out_shape=jax.ShapeDtypeStruct((tokens, HD), BF16),
        in_specs=[
            pl.BlockSpec((1, tile), lambda s: (0, s)),
            pl.BlockSpec((CTX, PAIR, HD), lambda s: (0, 0, 0)),
        ],
        out_specs=pl.BlockSpec((tile, HD), lambda s: (s, 0)),
        compiler_params=pltpu.CompilerParams(
            dimension_semantics=("arbitrary",), vmem_limit_bytes=32 << 20
        ),
        cost_estimate=pl.CostEstimate(
            flops=2 * tokens * 1024 * 512, bytes_accessed=2 << 20, transcendentals=0
        ),
        name="fetch",
    )(target, back)


def pack_kernel(
    ids_ref, q_ref, k_ref, v_ref,
    out_ref, dest_ref, at_ref,
    held, rows, row_hot, hot, slot_rows, over, done,
):
    step = pl.program_id(0)
    folds, per_step = out_ref.shape[0], out_ref.shape[1]
    tokens = ids_ref.shape[1]
    fold = CTX // folds

    @pl.when(step == 0)
    def _():
        copies = [
            pltpu.make_async_copy(ref, held.at[i], done.at[i])
            for i, ref in enumerate((q_ref, k_ref, v_ref))
        ]
        for copy in copies:
            copy.start()
        ids = ids_ref[...]
        rank, down = ranks_of(ids)
        dest, near = ids // LOCAL, ids % LOCAL
        dest_ref[...] = dest
        slots = lax.broadcasted_iota(jnp.int32, (PAIR, tokens), 0)
        group = slots // SLOTS
        to_dest = lax.broadcasted_iota(jnp.int32, (CTX, tokens), 0) == dest
        to_dest = jnp.where(to_dest, 1.0, 0.0).astype(BF16)
        equal = jnp.where(near == group, 1.0, 0.0).astype(BF16)
        less = jnp.where(near < group, 1.0, 0.0).astype(BF16)
        dims = (((1,), (1,)), ((), ()))
        count = lax.dot_general(to_dest, equal, dims, preferred_element_type=F32)
        start = lax.dot_general(to_dest, less, dims, preferred_element_type=F32)
        start_down = lax.dot_general(less, to_dest, dims, preferred_element_type=F32)
        first = jnp.dot(start_down.astype(BF16), to_dest, preferred_element_type=F32)
        first = jnp.sum(jnp.where(slots == near * SLOTS, first, 0.0), axis=0, keepdims=True)
        at = first.astype(jnp.int32) + rank
        at_ref[...] = at
        slot = lax.broadcasted_iota(jnp.int32, (CTX, PAIR), 1) % SLOTS
        slot = slot.astype(F32)
        slot_rows[...] = jnp.where(slot < count, start + slot, NO_ROW)
        most = jnp.max(start + count, axis=0, keepdims=True)
        most = jnp.max(most, axis=1, keepdims=True)
        over[...] = jnp.broadcast_to(jnp.where(most > ROOM, 1.0, 0.0), over.shape)
        index = lax.broadcasted_iota(jnp.int32, (ROOM, tokens), 0)
        row_hot[...] = jnp.where(index == at, 1.0, 0.0).astype(BF16)
        inside = []
        for column in down:
            parts = [
                (column >= f * fold * LOCAL) & (column < (f + 1) * fold * LOCAL)
                for f in range(folds)
            ]
            inside.append([jnp.where(part, 1.0, 0.0).astype(BF16) for part in parts])
        for i, copy in enumerate(copies):
            copy.wait()
            for j, parts in enumerate(inside):
                block = held[i, j * TILE : (j + 1) * TILE, :]
                for f, part in enumerate(parts):
                    low = (3 * f + i) * HD
                    rows[j * TILE : (j + 1) * TILE, low : low + HD] = block * part

    for i in range(per_step):
        mine = jnp.where(dest_ref[...] % fold == step * per_step + i, 1.0, 0.0)
        mine = jnp.broadcast_to(mine, (16, tokens)).astype(BF16)
        here = row_hot[...].reshape(ROOM // 16, 16, tokens) * mine[None]
        hot[i * ROOM : (i + 1) * ROOM, :] = here.reshape(ROOM, tokens)
    placed = jnp.dot(hot[...], rows[...], preferred_element_type=F32).astype(BF16)
    line = lax.broadcasted_iota(jnp.int32, (META, HD), 0)
    for f in range(folds):
        for part in range(3):
            low = (3 * f + part) * HD
            columns = placed[:, low : low + HD].reshape(per_step, ROOM, HD)
            out_ref[f, :, part * ROOM : (part + 1) * ROOM] = columns
        for i in range(per_step):
            mine = slot_rows[pl.ds(f * fold + step * per_step + i, 1), :]
            meta = jnp.where(line == 0, mine, jnp.where(line == 1, over[...], 0.0))
            out_ref[f, i, 3 * ROOM :] = meta.astype(BF16)


def pack(ids_row, queries, keys, values, per_step=8, folds=2):
    tokens = queries.shape[0]
    line = pl.BlockSpec((1, tokens), lambda s: (0, 0))
    anywhere = pl.BlockSpec(memory_space=pl.ANY)
    outgoing, dest, at = pl.pallas_call(
        pack_kernel,
        grid=(CTX // folds // per_step,),
        out_shape=(
            jax.ShapeDtypeStruct((folds, CTX // folds, CHUNK, HD), BF16),
            jax.ShapeDtypeStruct((1, tokens), jnp.int32),
            jax.ShapeDtypeStruct((1, tokens), jnp.int32),
        ),
        in_specs=[line, anywhere, anywhere, anywhere],
        out_specs=(
            pl.BlockSpec((folds, per_step, CHUNK, HD), lambda s: (0, s, 0, 0)),
            line,
            line,
        ),
        scratch_shapes=[
            pltpu.VMEM((3, tokens, HD), BF16),
            pltpu.VMEM((tokens, 3 * folds * HD), BF16),
            pltpu.VMEM((ROOM, tokens), BF16),
            pltpu.VMEM((per_step * ROOM, tokens), BF16),
            pltpu.VMEM((CTX, PAIR), F32),
            pltpu.VMEM((META, HD), F32),
            pltpu.SemaphoreType.DMA((3,)),
        ],
        compiler_params=pltpu.CompilerParams(
            dimension_semantics=("arbitrary",), vmem_limit_bytes=60 << 20
        ),
        cost_estimate=pl.CostEstimate(
            flops=2 * CTX * ROOM * tokens * 3 * HD, bytes_accessed=5 << 20, transcendentals=0
        ),
        name="pack",
    )(ids_row, queries, keys, values)
    return outgoing.reshape(CTX, CHUNK, HD), dest, at


def mix_kernel(recv_ref, old_ref, out_ref, sums_ref, over_ref, wide, mixed, total):
    sources = recv_ref.shape[0]
    members = sources * SLOTS
    lanes = lax.broadcasted_iota(jnp.int32, (PAIR, HD), 1).astype(F32)
    index = lax.broadcasted_iota(jnp.int32, (ROOM, PAIR), 0).astype(F32)
    first_lane = (lax.broadcasted_iota(jnp.int32, (16, HD), 1) == 0).astype(BF16)
    ones = jnp.ones((members, HD), BF16)
    dims = (((1,), (1,)), ((), ()))

    flags = jnp.max(recv_ref[:, 3 * ROOM :, :].astype(F32), axis=0)
    over_ref[0, 0] = jnp.max(flags[1:2, :]).astype(jnp.int32)

    def slot_row(source):
        return recv_ref[source, 3 * ROOM :, :].astype(F32)[0:1, :]

    def expand(source):
        down = jnp.transpose(jnp.broadcast_to(slot_row(source), (PAIR, PAIR)))
        take = jnp.where(down == lanes, 1.0, 0.0).astype(BF16)[:, 0:ROOM]
        parts = [recv_ref[source, i * ROOM : (i + 1) * ROOM, :] for i in range(3)]
        found = jnp.dot(take, jnp.concatenate(parts, axis=1), preferred_element_type=F32)
        mark = jnp.where((down == NO_ROW) & (lanes == 0.0), EMPTY, 0.0)
        keys = found[:, HD : 2 * HD]
        total[...] += keys
        wide[0, :, source] = found[:, 0:HD].reshape(LOCAL, SLOTS, HD)
        wide[1, :, source] = (keys + mark).reshape(LOCAL, SLOTS, HD)
        wide[2, :, source] = found[:, 2 * HD :].reshape(LOCAL, SLOTS, HD)

    def attend_one(cluster):
        q, k, v = (wide[i, cluster].reshape(members, HD).astype(BF16) for i in range(3))
        both = jnp.concatenate([q, first_lane], axis=0)
        both = lax.dot_general(both, k, dims, preferred_element_type=F32)
        present = both[members : members + 1] < 0.5 * EMPTY
        scores = jnp.where(present, both[0:members], NEG_FILL)
        weights = jnp.exp2((scores - jnp.max(scores, axis=1, keepdims=True)) * EXP2_SCALE)
        totals = jnp.dot(
            weights.astype(BF16), jnp.concatenate([v, ones], axis=1), preferred_element_type=F32
        )
        mixed[:, cluster] = (totals[:, 0:HD] / totals[:, HD:]).reshape(sources, SLOTS, HD)

    def compress(source):
        put = jnp.where(index == slot_row(source), 1.0, 0.0).astype(BF16)
        slots = mixed[source].reshape(PAIR, HD).astype(BF16)
        out_ref[source] = jnp.dot(put, slots, preferred_element_type=F32).astype(BF16)

    def each(body, count, unroll):
        def some(step, carry):
            for i in range(unroll):
                body(step * unroll + i)
            return carry

        lax.fori_loop(0, count // unroll, some, 0)

    total[...] = jnp.zeros_like(total)
    each(expand, sources, sources)
    member_sums = jnp.sum(total[...].reshape(LOCAL, SLOTS, HD), axis=1)
    sums_ref[...] = DECAY * old_ref[...] + (1.0 - DECAY) * member_sums
    each(attend_one, LOCAL, LOCAL)
    each(compress, sources, sources)


def mix(recv, old_sums):
    return pl.pallas_call(
        mix_kernel,
        out_shape=(
            jax.ShapeDtypeStruct((CTX, ROOM, HD), BF16),
            jax.ShapeDtypeStruct((LOCAL, HD), F32),
            jax.ShapeDtypeStruct((1, 1), jnp.int32),
        ),
        in_specs=[pl.BlockSpec(memory_space=pltpu.VMEM)] * 2,
        out_specs=(
            pl.BlockSpec(memory_space=pltpu.VMEM),
            pl.BlockSpec(memory_space=pltpu.VMEM),
            pl.BlockSpec(memory_space=pltpu.SMEM),
        ),
        scratch_shapes=[
            pltpu.VMEM((3, LOCAL, CTX, SLOTS, HD), F32),
            pltpu.VMEM((CTX, LOCAL, SLOTS, HD), F32),
            pltpu.VMEM((PAIR, HD), F32),
        ],
        compiler_params=pltpu.CompilerParams(vmem_limit_bytes=32 << 20),
        cost_estimate=pl.CostEstimate(
            flops=4 * LOCAL * 256 * 256 * HD,
            bytes_accessed=5 << 20,
            transcendentals=LOCAL * 256 * 256,
        ),
        name="mix",
    )(recv, old_sums)


def unpack_kernel(dest_ref, at_ref, back_ref, out_ref, table):
    tokens = out_ref.shape[0]

    @pl.when(pl.program_id(0) == 0)
    def _():
        for i in range(CTX):
            low, high = (i % 8) * PAIR, i // 8 * HD
            table[low : low + ROOM, high : high + HD] = back_ref[i]
            table[low + ROOM : low + PAIR, high : high + HD] = jnp.zeros((PAIR - ROOM, HD), BF16)

    lanes = lax.broadcasted_iota(jnp.int32, (TILE, PAIR), 1)

    def down(ref, j):
        here = ref[:, j * TILE : (j + 1) * TILE].astype(F32)
        return jnp.transpose(jnp.broadcast_to(here, (TILE, TILE))).astype(jnp.int32)

    for j in range(tokens // TILE):
        dest = down(dest_ref, j)
        slot = jnp.where(lanes == down(at_ref, j), 1.0, 0.0)
        hot = [jnp.where(dest % 8 == i, slot, 0.0).astype(BF16) for i in range(8)]
        found = jnp.dot(jnp.concatenate(hot, axis=1), table[...], preferred_element_type=F32)
        row = found[:, 0:HD]
        for i in range(1, CTX // 8):
            row = jnp.where(dest // 8 == i, found[:, i * HD : (i + 1) * HD], row)
        out_ref[j * TILE : (j + 1) * TILE, :] = row.astype(BF16)


def unpack(dest, at, back, tile=1024):
    tokens = dest.shape[1]
    line = pl.BlockSpec((1, tile), lambda s: (0, s))
    return pl.pallas_call(
        unpack_kernel,
        grid=(tokens // tile,),
        out_shape=jax.ShapeDtypeStruct((tokens, HD), BF16),
        in_specs=[line, line, pl.BlockSpec((CTX, ROOM, HD), lambda s: (0, 0, 0))],
        out_specs=pl.BlockSpec((tile, HD), lambda s: (s, 0)),
        scratch_shapes=[pltpu.VMEM((8 * PAIR, CTX // 8 * HD), BF16)],
        compiler_params=pltpu.CompilerParams(
            dimension_semantics=("arbitrary",), vmem_limit_bytes=32 << 20
        ),
        cost_estimate=pl.CostEstimate(
            flops=2 * tokens * 1024 * 512, bytes_accessed=2 << 20, transcendentals=0
        ),
        name="unpack",
    )(dest, at, back)


def project_kernel(heads_ref, w_ref, out_ref, *, columns):
    halves, blocks = w_ref.shape[0], w_ref.shape[1]
    each = heads_ref.shape[0] // halves
    left = [
        jnp.concatenate([heads_ref[c * each + i] for i in range(each)], axis=1)
        for c in range(halves)
    ]
    for low in range(0, blocks, columns):
        total = 0.0
        for c in range(halves):
            right = jnp.concatenate([w_ref[c, low + n] for n in range(columns)], axis=1)
            total = total + jnp.dot(left[c], right, preferred_element_type=F32)
        for n in range(columns):
            out_ref[low + n] = total[:, n * HD : (n + 1) * HD].astype(BF16)


def project(heads, w_all, columns=4):
    halves, blocks, depth, width = w_all.shape
    tokens = heads.shape[1]
    return pl.pallas_call(
        functools.partial(project_kernel, columns=columns),
        out_shape=jax.ShapeDtypeStruct((blocks, tokens, width), BF16),
        in_specs=[pl.BlockSpec(memory_space=pltpu.VMEM)] * 2,
        out_specs=pl.BlockSpec(memory_space=pltpu.VMEM),
        compiler_params=pltpu.CompilerParams(vmem_limit_bytes=32 << 20),
        cost_estimate=pl.CostEstimate(
            flops=2 * tokens * halves * depth * blocks * width,
            bytes_accessed=9 << 20,
            transcendentals=0,
        ),
        name="project",
    )(heads, w_all)


def over_ctx(chunks):
    return lax.all_to_all(chunks, "ctx", split_axis=0, concat_axis=0, tiled=True)


def on_device(queries, keys, values, cluster_ids, w_out, old_sums):
    hg_count = lax.axis_size("hg")
    tok_rows = queries.shape[0]
    half = w_out.shape[0] // 2
    w_half = lax.dynamic_slice_in_dim(w_out, lax.axis_index("ctx") % 2 * half, half)
    ids_row = cluster_ids[:, :, 0]
    outgoing, dest, at = pack(ids_row, queries, keys, values)
    chips = [list(range(2 * hg_count * i, 2 * hg_count * (i + 1))) for i in range(CTX // 2)]
    w_all = lax.all_gather(w_half, ("ctx", "hg"), axis_index_groups=chips)
    mixed_rows, sums, over = mix(over_ctx(outgoing), old_sums[0])

    def compact():
        return unpack(dest, at, over_ctx(mixed_rows)), sums

    def general():
        slots, target = place(ids_row, queries, keys, values)
        slot_rows, slot_sums = attend(over_ctx(slots), old_sums[0])
        return fetch(target, over_ctx(slot_rows)), slot_sums

    attention, centroid_sums = lax.cond(over[0, 0] > 0, general, compact)
    attention = attention.reshape(hg_count, tok_rows // hg_count, HD)
    all_heads = lax.all_to_all(attention, "hg", split_axis=0, concat_axis=0, tiled=True)
    w_all = w_all.reshape(2, hg_count, -1, w_out.shape[1])
    mixed = project(all_heads, w_all)
    projected = lax.all_to_all(mixed, "hg", split_axis=0, concat_axis=0, tiled=True)
    return (projected.reshape(tok_rows, w_out.shape[1]), centroid_sums[None])


def solution(mesh):
    placed = (
        P("ctx", "hg"),
        P("ctx", "hg"),
        P("ctx", "hg"),
        P("hg", "ctx", None),
        P(None, "hg"),
        P("hg", "ctx", None),
    )
    return jax.shard_map(
        on_device,
        mesh=mesh,
        in_specs=placed,
        out_specs=(P("ctx", "hg"), P("hg", "ctx", None)),
        check_vma=False,
    )
```

```python
import jax
import jax.numpy as jnp
from jax import lax
from jax.experimental import pallas as pl
from jax.experimental.pallas import tpu as pltpu
from jax.sharding import PartitionSpec as P

HD = 128
NCL = 512
SLOTS = 8
CTX = 32
LOCAL = NCL // CTX
PAIR = LOCAL * SLOTS
ROOM = 96
META = 8
CHUNK = 3 * ROOM + META
NO_ROW = 255.0
KEPT = 4
TILE = 128

DECAY = 0.9
NEG_FILL = -1e30
EMPTY = 1024.0

EXP2_SCALE = HD ** (-0.5) * 1.4426950408889634

F32 = jnp.float32
BF16 = jnp.bfloat16


def ranks_of(ids):
    wide = ids.astype(F32)
    before = lax.broadcasted_iota(jnp.int32, (TILE, TILE), 0) < lax.broadcasted_iota(
        jnp.int32, (TILE, TILE), 1
    )
    columns = [wide[:, i * TILE : (i + 1) * TILE] for i in range(ids.shape[1] // TILE)]
    down = [jnp.transpose(jnp.broadcast_to(c, (TILE, TILE))) for c in columns]
    ranks = []
    for j, column in enumerate(columns):
        here = jnp.broadcast_to(column, (TILE, TILE))
        same = jnp.where((down[j] == here) & before, 1.0, 0.0)
        for i in range(j):
            same = same + jnp.where(down[i] == here, 1.0, 0.0)
        ranks.append(jnp.sum(same, axis=0, keepdims=True))
    return jnp.concatenate(ranks, axis=1).astype(jnp.int32), down


def place_kernel(
    ids_ref, q_ref, k_ref, v_ref, out_ref, target_ref, rows, slot_hot, hot, dest_row
):
    step = pl.program_id(0)
    per_step = out_ref.shape[0]
    tokens = ids_ref.shape[1]

    @pl.when(step == 0)
    def _():
        ids = ids_ref[...]
        rank, _ = ranks_of(ids)
        target_ref[...] = ids * SLOTS + rank
        slot = (ids % LOCAL) * SLOTS + rank
        slots = lax.broadcasted_iota(jnp.int32, (PAIR, tokens), 0)
        slot_hot[...] = jnp.where(slots == slot, 1.0, 0.0).astype(BF16)
        dest_row[...] = ids // LOCAL
        rows[:, 0:HD] = k_ref[...]
        rows[:, HD : 2 * HD] = jnp.ones((tokens, HD), BF16)
        rows[:, 2 * HD : 3 * HD] = q_ref[...]
        rows[:, 3 * HD : 4 * HD] = v_ref[...]

    for i in range(per_step):
        mine = jnp.where(dest_row[...] == step * per_step + i, 1.0, 0.0)
        mine = jnp.broadcast_to(mine, (16, tokens)).astype(BF16)
        here = slot_hot[...].reshape(PAIR // 16, 16, tokens) * mine[None]
        hot[i * PAIR : (i + 1) * PAIR, :] = here.reshape(PAIR, tokens)
    shape = (per_step, PAIR, HD)
    keyed = jnp.dot(hot[...], rows[:, 0 : 2 * HD], preferred_element_type=F32)
    filled = keyed[:, HD : 2 * HD]
    first_lane = lax.broadcasted_iota(jnp.int32, filled.shape, 1) == 0
    marked = keyed[:, 0:HD] + jnp.where(first_lane, EMPTY * (1.0 - filled), 0.0)
    out_ref[:, 1] = marked.astype(BF16).reshape(shape)
    others = jnp.dot(hot[...], rows[:, 2 * HD : 4 * HD], preferred_element_type=F32)
    out_ref[:, 0] = others[:, 0:HD].astype(BF16).reshape(shape)
    out_ref[:, 2] = others[:, HD : 2 * HD].astype(BF16).reshape(shape)


def place(ids_row, queries, keys, values, per_step=8):
    tokens = queries.shape[0]
    whole = pl.BlockSpec((tokens, HD), lambda s: (0, 0))
    line = pl.BlockSpec((1, tokens), lambda s: (0, 0))
    return pl.pallas_call(
        place_kernel,
        grid_spec=pltpu.PrefetchScalarGridSpec(
            num_scalar_prefetch=0,
            grid=(CTX // per_step,),
            in_specs=[
                line,
                whole,
                whole,
                whole,
            ],
            out_specs=(
                pl.BlockSpec((per_step, 3, PAIR, HD), lambda s: (s, 0, 0, 0)),
                line,
            ),
            scratch_shapes=[
                pltpu.VMEM((tokens, 4 * HD), BF16),
                pltpu.VMEM((PAIR, tokens), BF16),
                pltpu.VMEM((per_step * PAIR, tokens), BF16),
                pltpu.VMEM((1, tokens), jnp.int32),
            ],
        ),
        out_shape=(
            jax.ShapeDtypeStruct((CTX, 3, PAIR, HD), BF16),
            jax.ShapeDtypeStruct((1, tokens), jnp.int32),
        ),
        compiler_params=pltpu.CompilerParams(
            dimension_semantics=("arbitrary",), vmem_limit_bytes=60 << 20
        ),
        cost_estimate=pl.CostEstimate(
            flops=2 * NCL * SLOTS * tokens * 4 * HD, bytes_accessed=5 << 20, transcendentals=0
        ),
        name="place",
    )(ids_row, queries, keys, values)


def attend_kernel(q_ref, k_ref, v_ref, old_ref, out_ref, sums_ref):
    step = pl.program_id(0)
    sources, block = q_ref.shape[0], q_ref.shape[2]
    count = block // SLOTS
    members = sources * SLOTS

    def split(ref):
        whole = ref[...].reshape(sources, block, HD).astype(F32)
        return [
            whole[:, i * SLOTS : (i + 1) * SLOTS].reshape(members, HD).astype(BF16)
            for i in range(count)
        ]

    first_lane = (lax.broadcasted_iota(jnp.int32, (16, HD), 1) == 0).astype(BF16)
    ones = jnp.ones((members, HD), BF16)
    dims = (((1,), (1,)), ((), ()))
    mixed, sums = [], []
    for q, k, v in zip(split(q_ref), split(k_ref), split(v_ref)):
        marks = lax.dot_general(first_lane, k, dims, preferred_element_type=F32)
        present = marks < 0.5 * EMPTY
        scores = lax.dot_general(q, k, dims, preferred_element_type=F32)
        scores = jnp.where(present[0:1], scores, NEG_FILL)
        weights = jnp.exp2((scores - jnp.max(scores, axis=1, keepdims=True)) * EXP2_SCALE)
        totals = jnp.dot(
            weights.astype(BF16), jnp.concatenate([v, ones], axis=1), preferred_element_type=F32
        )
        mixed.append((totals[:, 0:HD] / totals[:, HD:]).reshape(sources, SLOTS, HD))
        live = jnp.where(present, 1.0, 0.0).astype(BF16)
        sums.append(jnp.dot(live, k, preferred_element_type=F32)[0:1])
    out_ref[...] = jnp.concatenate(mixed, axis=1).astype(BF16)
    member_sums = jnp.concatenate(sums, axis=0)
    these = pl.ds(count * step, count)
    sums_ref[these, :] = DECAY * old_ref[these, :] + (1.0 - DECAY) * member_sums


def attend(slab, old_sums, count=4):
    def part(which):
        return pl.BlockSpec((CTX, 1, count * SLOTS, HD), lambda s: (0, which, s, 0))

    cell = pl.BlockSpec((LOCAL, HD), lambda s: (0, 0))
    return pl.pallas_call(
        attend_kernel,
        grid=(LOCAL // count,),
        out_shape=(
            jax.ShapeDtypeStruct((CTX, PAIR, HD), BF16),
            jax.ShapeDtypeStruct((LOCAL, HD), F32),
        ),
        in_specs=[part(0), part(1), part(2), cell],
        out_specs=(pl.BlockSpec((CTX, count * SLOTS, HD), lambda s: (0, s, 0)), cell),
        compiler_params=pltpu.CompilerParams(
            dimension_semantics=("arbitrary",), vmem_limit_bytes=32 << 20
        ),
        cost_estimate=pl.CostEstimate(
            flops=4 * LOCAL * 256 * 256 * HD,
            bytes_accessed=5 << 20,
            transcendentals=LOCAL * 256 * 256,
        ),
        name="attend",
    )(slab, slab, slab, old_sums)


def fetch_kernel(target_ref, back_ref, out_ref):
    tokens = out_ref.shape[0]
    lanes = lax.broadcasted_iota(jnp.int32, (TILE, PAIR), 1)
    for j in range(tokens // TILE):
        here = target_ref[:, j * TILE : (j + 1) * TILE].astype(F32)
        down = jnp.transpose(jnp.broadcast_to(here, (TILE, TILE))).astype(jnp.int32)
        dest = down // PAIR
        slot = jnp.where(lanes == down % PAIR, 1.0, 0.0)
        hot = [jnp.where(dest % 8 == i, slot, 0.0).astype(BF16) for i in range(8)]
        found = jnp.dot(
            jnp.concatenate(hot, axis=1),
            jnp.concatenate(
                [back_ref[8 * i : 8 * i + 8].reshape(8 * PAIR, HD) for i in range(CTX // 8)], axis=1
            ),
            preferred_element_type=F32,
        )
        row = found[:, 0:HD]
        for i in range(1, CTX // 8):
            row = jnp.where(dest // 8 == i, found[:, i * HD : (i + 1) * HD], row)
        out_ref[j * TILE : (j + 1) * TILE, :] = row.astype(BF16)


def fetch(target, back, tile=1024):
    tokens = target.shape[1]
    return pl.pallas_call(
        fetch_kernel,
        grid=(tokens // tile,),
        out_shape=jax.ShapeDtypeStruct((tokens, HD), BF16),
        in_specs=[
            pl.BlockSpec((1, tile), lambda s: (0, s)),
            pl.BlockSpec((CTX, PAIR, HD), lambda s: (0, 0, 0)),
        ],
        out_specs=pl.BlockSpec((tile, HD), lambda s: (s, 0)),
        compiler_params=pltpu.CompilerParams(
            dimension_semantics=("arbitrary",), vmem_limit_bytes=32 << 20
        ),
        cost_estimate=pl.CostEstimate(
            flops=2 * tokens * 1024 * 512, bytes_accessed=2 << 20, transcendentals=0
        ),
        name="fetch",
    )(target, back)


def pack_kernel(
    ids_ref, q_ref, k_ref, v_ref,
    sent_ref, code_ref,
    held, rows, row_hot, hot, slot_rows, out_ref, done, gone,
):
    folds = out_ref.shape[0]
    tokens = ids_ref.shape[1]
    fold = CTX // folds
    per_step = hot.shape[0] // ROOM
    copies = [
        pltpu.make_async_copy(ref, held.at[i], done.at[i])
        for i, ref in enumerate((q_ref, k_ref, v_ref))
    ]
    for copy in copies:
        copy.start()
    ids = ids_ref[...]
    rank, down = ranks_of(ids)
    dest, near = lax.shift_right_logical(ids, LOCAL.bit_length() - 1), ids & (LOCAL - 1)
    slots = lax.broadcasted_iota(jnp.int32, (PAIR, tokens), 0)
    group = lax.shift_right_logical(slots, SLOTS.bit_length() - 1)
    to_dest = lax.broadcasted_iota(jnp.int32, (CTX, tokens), 0) == dest
    to_dest = jnp.where(to_dest, 1.0, 0.0).astype(BF16)
    equal = jnp.where(near == group, 1.0, 0.0).astype(BF16)
    less = jnp.where(near < group, 1.0, 0.0).astype(BF16)
    dims = (((1,), (1,)), ((), ()))
    count = lax.dot_general(to_dest, equal, dims, preferred_element_type=F32)
    start = lax.dot_general(to_dest, less, dims, preferred_element_type=F32)
    start_down = lax.dot_general(less, to_dest, dims, preferred_element_type=F32)
    first = jnp.dot(start_down.astype(BF16), to_dest, preferred_element_type=F32)
    first = jnp.sum(jnp.where(slots == near * SLOTS, first, 0.0), axis=0, keepdims=True)
    at = first.astype(jnp.int32) + rank
    code_ref[...] = dest * PAIR + at
    slot = lax.broadcasted_iota(jnp.int32, (CTX, PAIR), 1) & (SLOTS - 1)
    slot = slot.astype(F32)
    slot_rows[...] = jnp.where(slot < count, start + slot, NO_ROW)
    most = jnp.max(start + count, axis=0, keepdims=True)
    most = jnp.max(most, axis=1, keepdims=True)
    over = jnp.where(most > ROOM, 1.0, 0.0)
    index = lax.broadcasted_iota(jnp.int32, (ROOM, tokens), 0)
    row_hot[...] = jnp.where(index == at, 1.0, 0.0).astype(BF16)
    inside = []
    for column in down:
        parts = [
            (column >= f * fold * LOCAL) & (column < (f + 1) * fold * LOCAL)
            for f in range(folds)
        ]
        inside.append([jnp.where(part, 1.0, 0.0).astype(BF16) for part in parts])
    for i, copy in enumerate(copies):
        copy.wait()
        for j, parts in enumerate(inside):
            block = held[i, j * TILE : (j + 1) * TILE, :]
            for f, part in enumerate(parts):
                low = (3 * f + i) * HD
                rows[j * TILE : (j + 1) * TILE, low : low + HD] = block * part

    near_dest = dest & (fold - 1)
    line = lax.broadcasted_iota(jnp.int32, (META, HD), 0)
    leaving = []
    for step in range(fold // per_step):
        these = slice(step * per_step, (step + 1) * per_step)
        for i in range(per_step):
            mine = jnp.where(near_dest == step * per_step + i, 1.0, 0.0)
            mine = jnp.broadcast_to(mine, (16, tokens)).astype(BF16)
            here = row_hot[...].reshape(ROOM // 16, 16, tokens) * mine[None]
            hot[i * ROOM : (i + 1) * ROOM, :] = here.reshape(ROOM, tokens)
        placed = jnp.dot(hot[...], rows[...], preferred_element_type=F32).astype(BF16)
        for f in range(folds):
            for part in range(3):
                low = (3 * f + part) * HD
                columns = placed[:, low : low + HD].reshape(per_step, ROOM, HD)
                out_ref[f, these, part * ROOM : (part + 1) * ROOM] = columns
            for i in range(step * per_step, (step + 1) * per_step):
                mine = slot_rows[f * fold + i : f * fold + i + 1, :]
                meta = jnp.where(line == 0, mine, jnp.where(line == 1, over, 0.0))
                out_ref[f, i, 3 * ROOM :] = meta.astype(BF16)
            there = pl.ds(step * per_step, per_step)
            leaving.append(
                pltpu.make_async_copy(
                    out_ref.at[f, there], sent_ref.at[f, there], gone.at[f, step]
                )
            )
            leaving[-1].start()
    for copy in leaving:
        copy.wait()


def pack(ids_row, queries, keys, values, per_step=4, folds=2):
    tokens = queries.shape[0]
    vmem = pl.BlockSpec(memory_space=pltpu.VMEM)
    hbm = pl.BlockSpec(memory_space=pltpu.HBM)
    outgoing, code = pl.pallas_call(
        pack_kernel,
        out_shape=(
            jax.ShapeDtypeStruct((folds, CTX // folds, CHUNK, HD), BF16),
            jax.ShapeDtypeStruct((1, tokens), jnp.int32),
        ),
        in_specs=[vmem, hbm, hbm, hbm],
        out_specs=(hbm, vmem),
        scratch_shapes=[
            pltpu.VMEM((3, tokens, HD), BF16),
            pltpu.VMEM((tokens, 3 * folds * HD), BF16),
            pltpu.VMEM((ROOM, tokens), BF16),
            pltpu.VMEM((per_step * ROOM, tokens), BF16),
            pltpu.VMEM((CTX, PAIR), F32),
            pltpu.VMEM((folds, CTX // folds, CHUNK, HD), BF16),
            pltpu.SemaphoreType.DMA((3,)),
            pltpu.SemaphoreType.DMA((folds, CTX // folds // per_step)),
        ],
        compiler_params=pltpu.CompilerParams(vmem_limit_bytes=60 << 20),
        cost_estimate=pl.CostEstimate(
            flops=2 * CTX * ROOM * tokens * 3 * HD, bytes_accessed=5 << 20, transcendentals=0
        ),
        name="pack",
    )(ids_row, queries, keys, values)
    return outgoing.reshape(CTX, CHUNK, HD), code


def mix_kernel(recv_ref, old_ref, out_ref, sums_ref, over_ref, wide, mixed, total):
    sources = recv_ref.shape[0]
    members = sources * SLOTS
    lanes = lax.broadcasted_iota(jnp.int32, (PAIR, HD), 1).astype(F32)
    index = lax.broadcasted_iota(jnp.int32, (ROOM, PAIR), 0).astype(F32)
    first_lane = (lax.broadcasted_iota(jnp.int32, (16, HD), 1) == 0).astype(BF16)
    ones = jnp.ones((members, HD), BF16)
    dims = (((1,), (1,)), ((), ()))

    flags = jnp.max(recv_ref[:, 3 * ROOM :, :].astype(F32), axis=0)
    over_ref[0, 0] = jnp.max(flags[1:2, :]).astype(jnp.int32)

    def slot_row(source):
        return recv_ref[source, 3 * ROOM :, :].astype(F32)[0:1, :]

    def expand(source):
        down = jnp.transpose(jnp.broadcast_to(slot_row(source), (PAIR, PAIR)))
        take = jnp.where(down == lanes, 1.0, 0.0).astype(BF16)[:, 0:ROOM]
        parts = [recv_ref[source, i * ROOM : (i + 1) * ROOM, :] for i in range(3)]
        found = jnp.dot(take, jnp.concatenate(parts, axis=1), preferred_element_type=F32)
        mark = jnp.where((down == NO_ROW) & (lanes == 0.0), EMPTY, 0.0)
        keys = found[:, HD : 2 * HD]
        total[...] += keys
        wide[0, :, source] = found[:, 0:HD].reshape(LOCAL, SLOTS, HD)
        wide[1, :, source] = (keys + mark).reshape(LOCAL, SLOTS, HD)
        wide[2, :, source] = found[:, 2 * HD :].reshape(LOCAL, SLOTS, HD)

    def attend_one(cluster):
        q, k, v = (wide[i, cluster].reshape(members, HD).astype(BF16) for i in range(3))
        both = jnp.concatenate([q, first_lane], axis=0)
        both = lax.dot_general(both, k, dims, preferred_element_type=F32)
        present = both[members : members + 1] < 0.5 * EMPTY
        scores = jnp.where(present, both[0:members], NEG_FILL)
        weights = jnp.exp2((scores - jnp.max(scores, axis=1, keepdims=True)) * EXP2_SCALE)
        totals = jnp.dot(
            weights.astype(BF16), jnp.concatenate([v, ones], axis=1), preferred_element_type=F32
        )
        mixed[:, cluster] = (totals[:, 0:HD] / totals[:, HD:]).reshape(sources, SLOTS, HD)

    def compress(source):
        put = jnp.where(index == slot_row(source), 1.0, 0.0).astype(BF16)
        slots = mixed[source].reshape(PAIR, HD).astype(BF16)
        out_ref[source] = jnp.dot(put, slots, preferred_element_type=F32).astype(BF16)

    def each(body, count, unroll):
        def some(step, carry):
            for i in range(unroll):
                body(step * unroll + i)
            return carry

        lax.fori_loop(0, count // unroll, some, 0)

    total[...] = jnp.zeros_like(total)
    each(expand, sources, sources)
    member_sums = jnp.sum(total[...].reshape(LOCAL, SLOTS, HD), axis=1)
    sums_ref[...] = DECAY * old_ref[...] + (1.0 - DECAY) * member_sums
    each(attend_one, LOCAL, LOCAL)
    each(compress, sources, sources)


def mix(recv, old_sums):
    return pl.pallas_call(
        mix_kernel,
        out_shape=(
            jax.ShapeDtypeStruct((CTX, ROOM, HD), BF16),
            jax.ShapeDtypeStruct((LOCAL, HD), F32),
            jax.ShapeDtypeStruct((1, 1), jnp.int32),
        ),
        in_specs=[pl.BlockSpec(memory_space=pltpu.VMEM)] * 2,
        out_specs=(
            pl.BlockSpec(memory_space=pltpu.VMEM),
            pl.BlockSpec(memory_space=pltpu.VMEM),
            pl.BlockSpec(memory_space=pltpu.SMEM),
        ),
        scratch_shapes=[
            pltpu.VMEM((3, LOCAL, CTX, SLOTS, HD), F32),
            pltpu.VMEM((CTX, LOCAL, SLOTS, HD), F32),
            pltpu.VMEM((PAIR, HD), F32),
        ],
        compiler_params=pltpu.CompilerParams(vmem_limit_bytes=32 << 20),
        cost_estimate=pl.CostEstimate(
            flops=4 * LOCAL * 256 * 256 * HD,
            bytes_accessed=5 << 20,
            transcendentals=LOCAL * 256 * 256,
        ),
        name="mix",
    )(recv, old_sums)


def unpack_kernel(code_ref, back_ref, out_ref, table):
    tokens = out_ref.shape[0]
    groups = table.shape[0] // PAIR

    @pl.when(pl.program_id(0) == 0)
    def _():
        for i in range(CTX):
            low, high = (i % groups) * PAIR, i // groups * HD
            table[low : low + ROOM, high : high + HD] = back_ref[i]
            table[low + ROOM : low + PAIR, high : high + HD] = jnp.zeros((PAIR - ROOM, HD), BF16)

    lanes = lax.broadcasted_iota(jnp.int32, (TILE, PAIR), 1)
    for j in range(tokens // TILE):
        here = code_ref[:, j * TILE : (j + 1) * TILE].astype(F32)
        down = jnp.transpose(jnp.broadcast_to(here, (TILE, TILE))).astype(jnp.int32)
        inner = down & (groups * PAIR - 1)
        outer = lax.shift_right_logical(down, (groups * PAIR).bit_length() - 1)
        hot = [jnp.where(inner == lanes + i * PAIR, 1.0, 0.0).astype(BF16) for i in range(groups)]
        found = jnp.dot(jnp.concatenate(hot, axis=1), table[...], preferred_element_type=F32)
        row = found[:, 0:HD]
        for i in range(1, CTX // groups):
            row = jnp.where(outer == i, found[:, i * HD : (i + 1) * HD], row)
        out_ref[j * TILE : (j + 1) * TILE, :] = row.astype(BF16)


def unpack(code, back, tile=2048, groups=8):
    tokens = code.shape[1]
    return pl.pallas_call(
        unpack_kernel,
        grid=(tokens // tile,),
        out_shape=jax.ShapeDtypeStruct((tokens, HD), BF16),
        in_specs=[
            pl.BlockSpec((1, tile), lambda s: (0, s)),
            pl.BlockSpec((CTX, ROOM, HD), lambda s: (0, 0, 0)),
        ],
        out_specs=pl.BlockSpec((tile, HD), lambda s: (s, 0)),
        scratch_shapes=[pltpu.VMEM((groups * PAIR, CTX // groups * HD), BF16)],
        compiler_params=pltpu.CompilerParams(
            dimension_semantics=("arbitrary",), vmem_limit_bytes=32 << 20
        ),
        cost_estimate=pl.CostEstimate(
            flops=2 * tokens * 1024 * 512, bytes_accessed=2 << 20, transcendentals=0
        ),
        name="unpack",
    )(code, back)


def hold_kernel(w_ref, out_ref, done):
    count = out_ref.shape[1]
    copies = [
        pltpu.make_async_copy(w_ref.at[c, pl.ds(0, count)], out_ref.at[c], done.at[c])
        for c in range(w_ref.shape[0])
    ]
    for copy in copies:
        copy.start()
    for copy in copies:
        copy.wait()


def hold(w_all, count=KEPT):
    halves, _, depth, width = w_all.shape
    return pl.pallas_call(
        hold_kernel,
        out_shape=jax.ShapeDtypeStruct((halves, count, depth, width), w_all.dtype),
        in_specs=[pl.BlockSpec(memory_space=pltpu.HBM)],
        out_specs=pl.BlockSpec(memory_space=pltpu.VMEM),
        scratch_shapes=[pltpu.SemaphoreType.DMA((halves,))],
        compiler_params=pltpu.CompilerParams(vmem_limit_bytes=8 << 20),
        cost_estimate=pl.CostEstimate(flops=0, bytes_accessed=16 << 20, transcendentals=0),
        name="hold",
    )(w_all)


def project_kernel(heads_ref, kept_ref, w_ref, out_ref, held, done):
    halves, steps, columns = held.shape[1], held.shape[0], held.shape[2]
    first = kept_ref.shape[1]
    each = heads_ref.shape[0] // halves
    copies = [
        [
            pltpu.make_async_copy(
                w_ref.at[c, pl.ds(first + p * columns, columns)], held.at[p, c], done.at[p, c]
            )
            for c in range(halves)
        ]
        for p in range(steps)
    ]
    for pair in copies:
        for copy in pair:
            copy.start()
    left = [
        jnp.concatenate([heads_ref[c * each + i] for i in range(each)], axis=1)
        for c in range(halves)
    ]

    def multiply(parts, low):
        total = 0.0
        for c, blocks in enumerate(parts):
            right = jnp.concatenate(blocks, axis=1)
            total = total + jnp.dot(left[c], right, preferred_element_type=F32)
        for n in range(len(parts[0])):
            out_ref[low + n] = total[:, n * HD : (n + 1) * HD].astype(BF16)

    multiply([[kept_ref[c, n] for n in range(first)] for c in range(halves)], 0)
    for p, pair in enumerate(copies):
        for copy in pair:
            copy.wait()
        multiply(
            [[held[p, c, n] for n in range(columns)] for c in range(halves)], first + p * columns
        )


def project(heads, kept, w_all, columns=4):
    halves, blocks, depth, width = w_all.shape
    tokens = heads.shape[1]
    steps = (blocks - kept.shape[1]) // columns
    vmem = pl.BlockSpec(memory_space=pltpu.VMEM)
    return pl.pallas_call(
        project_kernel,
        out_shape=jax.ShapeDtypeStruct((blocks, tokens, width), BF16),
        in_specs=[vmem, vmem, pl.BlockSpec(memory_space=pltpu.HBM)],
        out_specs=vmem,
        scratch_shapes=[
            pltpu.VMEM((steps, halves, columns, depth, width), BF16),
            pltpu.SemaphoreType.DMA((steps, halves)),
        ],
        compiler_params=pltpu.CompilerParams(vmem_limit_bytes=48 << 20),
        cost_estimate=pl.CostEstimate(
            flops=2 * tokens * halves * depth * blocks * width,
            bytes_accessed=9 << 20,
            transcendentals=0,
        ),
        name="project",
    )(heads, kept, w_all)


def over_ctx(chunks):
    return lax.all_to_all(chunks, "ctx", split_axis=0, concat_axis=0, tiled=True)


def on_device(queries, keys, values, cluster_ids, w_out, old_sums):
    hg_count = lax.axis_size("hg")
    tok_rows = queries.shape[0]
    half = w_out.shape[0] // 2
    w_half = lax.dynamic_slice_in_dim(w_out, lax.axis_index("ctx") % 2 * half, half)
    ids_row = cluster_ids[:, :, 0]
    outgoing, code = pack(ids_row, queries, keys, values)
    chips = [list(range(2 * hg_count * i, 2 * hg_count * (i + 1))) for i in range(CTX // 2)]
    w_all = lax.all_gather(w_half, ("ctx", "hg"), axis_index_groups=chips)
    mixed_rows, sums, over = mix(over_ctx(outgoing), old_sums[0])

    def compact():
        return unpack(code, over_ctx(mixed_rows)), sums

    def general():
        slots, target = place(ids_row, queries, keys, values)
        slot_rows, slot_sums = attend(over_ctx(slots), old_sums[0])
        return fetch(target, over_ctx(slot_rows)), slot_sums

    attention, centroid_sums = lax.cond(over[0, 0] > 0, general, compact)
    attention = attention.reshape(hg_count, tok_rows // hg_count, HD)
    all_heads = lax.all_to_all(attention, "hg", split_axis=0, concat_axis=0, tiled=True)
    w_all = w_all.reshape(2, hg_count, -1, w_out.shape[1])
    mixed = project(all_heads, hold(w_all), w_all)
    projected = lax.all_to_all(mixed, "hg", split_axis=0, concat_axis=0, tiled=True)
    return (projected.reshape(tok_rows, w_out.shape[1]), centroid_sums[None])


def solution(mesh):
    placed = (
        P("ctx", "hg"),
        P("ctx", "hg"),
        P("ctx", "hg"),
        P("hg", "ctx", None),
        P(None, "hg"),
        P("hg", "ctx", None),
    )
    return jax.shard_map(
        on_device,
        mesh=mesh,
        in_specs=placed,
        out_specs=(P("ctx", "hg"), P("hg", "ctx", None)),
        check_vma=False,
    )
```

```python
import jax
import jax.numpy as jnp
from jax import lax
from jax.experimental import pallas as pl
from jax.experimental.pallas import tpu as pltpu
from jax.sharding import PartitionSpec as P

HD = 128
NCL = 512
SLOTS = 8
CTX = 32
LOCAL = NCL // CTX
PAIR = LOCAL * SLOTS
ROOM = 96
META = 8
CHUNK = 3 * ROOM + META
NO_ROW = 255.0
KEPT = 4
TILE = 128

DECAY = 0.9
NEG_FILL = -1e30
EMPTY = 1024.0

EXP2_SCALE = HD ** (-0.5) * 1.4426950408889634

F32 = jnp.float32
BF16 = jnp.bfloat16


def ranks_of(ids):
    wide = ids.astype(F32)
    before = lax.broadcasted_iota(jnp.int32, (TILE, TILE), 0) < lax.broadcasted_iota(
        jnp.int32, (TILE, TILE), 1
    )
    columns = [wide[:, i * TILE : (i + 1) * TILE] for i in range(ids.shape[1] // TILE)]
    down = [jnp.transpose(jnp.broadcast_to(c, (TILE, TILE))) for c in columns]
    ranks = []
    for j, column in enumerate(columns):
        here = jnp.broadcast_to(column, (TILE, TILE))
        same = jnp.where((down[j] == here) & before, 1.0, 0.0)
        for i in range(j):
            same = same + jnp.where(down[i] == here, 1.0, 0.0)
        ranks.append(jnp.sum(same, axis=0, keepdims=True))
    return jnp.concatenate(ranks, axis=1).astype(jnp.int32), down


def place_kernel(
    ids_ref, q_ref, k_ref, v_ref, out_ref, target_ref, rows, slot_hot, hot, dest_row
):
    step = pl.program_id(0)
    per_step = out_ref.shape[0]
    tokens = ids_ref.shape[1]

    @pl.when(step == 0)
    def _():
        ids = ids_ref[...]
        rank, _ = ranks_of(ids)
        target_ref[...] = ids * SLOTS + rank
        slot = (ids % LOCAL) * SLOTS + rank
        slots = lax.broadcasted_iota(jnp.int32, (PAIR, tokens), 0)
        slot_hot[...] = jnp.where(slots == slot, 1.0, 0.0).astype(BF16)
        dest_row[...] = ids // LOCAL
        rows[:, 0:HD] = k_ref[...]
        rows[:, HD : 2 * HD] = jnp.ones((tokens, HD), BF16)
        rows[:, 2 * HD : 3 * HD] = q_ref[...]
        rows[:, 3 * HD : 4 * HD] = v_ref[...]

    for i in range(per_step):
        mine = jnp.where(dest_row[...] == step * per_step + i, 1.0, 0.0)
        mine = jnp.broadcast_to(mine, (16, tokens)).astype(BF16)
        here = slot_hot[...].reshape(PAIR // 16, 16, tokens) * mine[None]
        hot[i * PAIR : (i + 1) * PAIR, :] = here.reshape(PAIR, tokens)
    shape = (per_step, PAIR, HD)
    keyed = jnp.dot(hot[...], rows[:, 0 : 2 * HD], preferred_element_type=F32)
    filled = keyed[:, HD : 2 * HD]
    first_lane = lax.broadcasted_iota(jnp.int32, filled.shape, 1) == 0
    marked = keyed[:, 0:HD] + jnp.where(first_lane, EMPTY * (1.0 - filled), 0.0)
    out_ref[:, 1] = marked.astype(BF16).reshape(shape)
    others = jnp.dot(hot[...], rows[:, 2 * HD : 4 * HD], preferred_element_type=F32)
    out_ref[:, 0] = others[:, 0:HD].astype(BF16).reshape(shape)
    out_ref[:, 2] = others[:, HD : 2 * HD].astype(BF16).reshape(shape)


def place(ids_row, queries, keys, values, per_step=8):
    tokens = queries.shape[0]
    whole = pl.BlockSpec((tokens, HD), lambda s: (0, 0))
    line = pl.BlockSpec((1, tokens), lambda s: (0, 0))
    return pl.pallas_call(
        place_kernel,
        grid_spec=pltpu.PrefetchScalarGridSpec(
            num_scalar_prefetch=0,
            grid=(CTX // per_step,),
            in_specs=[
                line,
                whole,
                whole,
                whole,
            ],
            out_specs=(
                pl.BlockSpec((per_step, 3, PAIR, HD), lambda s: (s, 0, 0, 0)),
                line,
            ),
            scratch_shapes=[
                pltpu.VMEM((tokens, 4 * HD), BF16),
                pltpu.VMEM((PAIR, tokens), BF16),
                pltpu.VMEM((per_step * PAIR, tokens), BF16),
                pltpu.VMEM((1, tokens), jnp.int32),
            ],
        ),
        out_shape=(
            jax.ShapeDtypeStruct((CTX, 3, PAIR, HD), BF16),
            jax.ShapeDtypeStruct((1, tokens), jnp.int32),
        ),
        compiler_params=pltpu.CompilerParams(
            dimension_semantics=("arbitrary",), vmem_limit_bytes=60 << 20
        ),
        cost_estimate=pl.CostEstimate(
            flops=2 * NCL * SLOTS * tokens * 4 * HD, bytes_accessed=5 << 20, transcendentals=0
        ),
        name="place",
    )(ids_row, queries, keys, values)


def attend_kernel(q_ref, k_ref, v_ref, old_ref, out_ref, sums_ref):
    step = pl.program_id(0)
    sources, block = q_ref.shape[0], q_ref.shape[2]
    count = block // SLOTS
    members = sources * SLOTS

    def split(ref):
        whole = ref[...].reshape(sources, block, HD).astype(F32)
        return [
            whole[:, i * SLOTS : (i + 1) * SLOTS].reshape(members, HD).astype(BF16)
            for i in range(count)
        ]

    first_lane = (lax.broadcasted_iota(jnp.int32, (16, HD), 1) == 0).astype(BF16)
    ones = jnp.ones((members, HD), BF16)
    dims = (((1,), (1,)), ((), ()))
    mixed, sums = [], []
    for q, k, v in zip(split(q_ref), split(k_ref), split(v_ref)):
        marks = lax.dot_general(first_lane, k, dims, preferred_element_type=F32)
        present = marks < 0.5 * EMPTY
        scores = lax.dot_general(q, k, dims, preferred_element_type=F32)
        scores = jnp.where(present[0:1], scores, NEG_FILL)
        weights = jnp.exp2((scores - jnp.max(scores, axis=1, keepdims=True)) * EXP2_SCALE)
        totals = jnp.dot(
            weights.astype(BF16), jnp.concatenate([v, ones], axis=1), preferred_element_type=F32
        )
        mixed.append((totals[:, 0:HD] / totals[:, HD:]).reshape(sources, SLOTS, HD))
        live = jnp.where(present, 1.0, 0.0).astype(BF16)
        sums.append(jnp.dot(live, k, preferred_element_type=F32)[0:1])
    out_ref[...] = jnp.concatenate(mixed, axis=1).astype(BF16)
    member_sums = jnp.concatenate(sums, axis=0)
    these = pl.ds(count * step, count)
    sums_ref[these, :] = DECAY * old_ref[these, :] + (1.0 - DECAY) * member_sums


def attend(slab, old_sums, count=4):
    def part(which):
        return pl.BlockSpec((CTX, 1, count * SLOTS, HD), lambda s: (0, which, s, 0))

    cell = pl.BlockSpec((LOCAL, HD), lambda s: (0, 0))
    return pl.pallas_call(
        attend_kernel,
        grid=(LOCAL // count,),
        out_shape=(
            jax.ShapeDtypeStruct((CTX, PAIR, HD), BF16),
            jax.ShapeDtypeStruct((LOCAL, HD), F32),
        ),
        in_specs=[part(0), part(1), part(2), cell],
        out_specs=(pl.BlockSpec((CTX, count * SLOTS, HD), lambda s: (0, s, 0)), cell),
        compiler_params=pltpu.CompilerParams(
            dimension_semantics=("arbitrary",), vmem_limit_bytes=32 << 20
        ),
        cost_estimate=pl.CostEstimate(
            flops=4 * LOCAL * 256 * 256 * HD,
            bytes_accessed=5 << 20,
            transcendentals=LOCAL * 256 * 256,
        ),
        name="attend",
    )(slab, slab, slab, old_sums)


def fetch_kernel(target_ref, back_ref, out_ref):
    tokens = out_ref.shape[0]
    lanes = lax.broadcasted_iota(jnp.int32, (TILE, PAIR), 1)
    for j in range(tokens // TILE):
        here = target_ref[:, j * TILE : (j + 1) * TILE].astype(F32)
        down = jnp.transpose(jnp.broadcast_to(here, (TILE, TILE))).astype(jnp.int32)
        dest = down // PAIR
        slot = jnp.where(lanes == down % PAIR, 1.0, 0.0)
        hot = [jnp.where(dest % 8 == i, slot, 0.0).astype(BF16) for i in range(8)]
        found = jnp.dot(
            jnp.concatenate(hot, axis=1),
            jnp.concatenate(
                [back_ref[8 * i : 8 * i + 8].reshape(8 * PAIR, HD) for i in range(CTX // 8)], axis=1
            ),
            preferred_element_type=F32,
        )
        row = found[:, 0:HD]
        for i in range(1, CTX // 8):
            row = jnp.where(dest // 8 == i, found[:, i * HD : (i + 1) * HD], row)
        out_ref[j * TILE : (j + 1) * TILE, :] = row.astype(BF16)


def fetch(target, back, tile=1024):
    tokens = target.shape[1]
    return pl.pallas_call(
        fetch_kernel,
        grid=(tokens // tile,),
        out_shape=jax.ShapeDtypeStruct((tokens, HD), BF16),
        in_specs=[
            pl.BlockSpec((1, tile), lambda s: (0, s)),
            pl.BlockSpec((CTX, PAIR, HD), lambda s: (0, 0, 0)),
        ],
        out_specs=pl.BlockSpec((tile, HD), lambda s: (s, 0)),
        compiler_params=pltpu.CompilerParams(
            dimension_semantics=("arbitrary",), vmem_limit_bytes=32 << 20
        ),
        cost_estimate=pl.CostEstimate(
            flops=2 * tokens * 1024 * 512, bytes_accessed=2 << 20, transcendentals=0
        ),
        name="fetch",
    )(target, back)


def pack_kernel(
    ids_ref, q_ref, k_ref, v_ref,
    sent_ref, code_ref,
    held, rows, row_hot, hot, slot_rows, out_ref, done, gone,
):
    folds = out_ref.shape[0]
    tokens = ids_ref.shape[1]
    fold = CTX // folds
    per_step = hot.shape[0] // ROOM
    copies = [
        pltpu.make_async_copy(ref, held.at[i], done.at[i])
        for i, ref in enumerate((q_ref, k_ref, v_ref))
    ]
    for copy in copies:
        copy.start()
    ids = ids_ref[...]
    rank, down = ranks_of(ids)
    dest, near = lax.shift_right_logical(ids, LOCAL.bit_length() - 1), ids & (LOCAL - 1)
    slots = lax.broadcasted_iota(jnp.int32, (PAIR, tokens), 0)
    group = lax.shift_right_logical(slots, SLOTS.bit_length() - 1)
    to_dest = lax.broadcasted_iota(jnp.int32, (CTX, tokens), 0) == dest
    to_dest = jnp.where(to_dest, 1.0, 0.0).astype(BF16)
    equal = jnp.where(near == group, 1.0, 0.0).astype(BF16)
    less = jnp.where(near < group, 1.0, 0.0).astype(BF16)
    dims = (((1,), (1,)), ((), ()))
    count = lax.dot_general(to_dest, equal, dims, preferred_element_type=F32)
    start = lax.dot_general(to_dest, less, dims, preferred_element_type=F32)
    start_down = lax.dot_general(less, to_dest, dims, preferred_element_type=F32)
    first = jnp.dot(start_down.astype(BF16), to_dest, preferred_element_type=F32)
    first = jnp.sum(jnp.where(slots == near * SLOTS, first, 0.0), axis=0, keepdims=True)
    at = first.astype(jnp.int32) + rank
    code_ref[...] = dest * PAIR + at
    slot = lax.broadcasted_iota(jnp.int32, (CTX, PAIR), 1) & (SLOTS - 1)
    slot = slot.astype(F32)
    slot_rows[...] = jnp.where(slot < count, start + slot, NO_ROW)
    most = jnp.max(start + count, axis=0, keepdims=True)
    most = jnp.max(most, axis=1, keepdims=True)
    over = jnp.where(most > ROOM, 1.0, 0.0)
    index = lax.broadcasted_iota(jnp.int32, (ROOM, tokens), 0)
    row_hot[...] = jnp.where(index == at, 1.0, 0.0).astype(BF16)
    inside = []
    for column in down:
        parts = [
            (column >= f * fold * LOCAL) & (column < (f + 1) * fold * LOCAL)
            for f in range(folds)
        ]
        inside.append([jnp.where(part, 1.0, 0.0).astype(BF16) for part in parts])
    for i, copy in enumerate(copies):
        copy.wait()
        for j, parts in enumerate(inside):
            block = held[i, j * TILE : (j + 1) * TILE, :]
            for f, part in enumerate(parts):
                low = (3 * f + i) * HD
                rows[j * TILE : (j + 1) * TILE, low : low + HD] = block * part

    near_dest = dest & (fold - 1)
    line = lax.broadcasted_iota(jnp.int32, (META, HD), 0)
    leaving = []
    for step in range(fold // per_step):
        these = slice(step * per_step, (step + 1) * per_step)
        for i in range(per_step):
            mine = jnp.where(near_dest == step * per_step + i, 1.0, 0.0)
            mine = jnp.broadcast_to(mine, (16, tokens)).astype(BF16)
            here = row_hot[...].reshape(ROOM // 16, 16, tokens) * mine[None]
            hot[i * ROOM : (i + 1) * ROOM, :] = here.reshape(ROOM, tokens)
        placed = jnp.dot(hot[...], rows[...], preferred_element_type=F32).astype(BF16)
        for f in range(folds):
            for part in range(3):
                low = (3 * f + part) * HD
                columns = placed[:, low : low + HD].reshape(per_step, ROOM, HD)
                out_ref[f, these, part * ROOM : (part + 1) * ROOM] = columns
            for i in range(step * per_step, (step + 1) * per_step):
                mine = slot_rows[f * fold + i : f * fold + i + 1, :]
                meta = jnp.where(line == 0, mine, jnp.where(line == 1, over, 0.0))
                out_ref[f, i, 3 * ROOM :] = meta.astype(BF16)
            there = pl.ds(step * per_step, per_step)
            leaving.append(
                pltpu.make_async_copy(
                    out_ref.at[f, there], sent_ref.at[f, there], gone.at[f, step]
                )
            )
            leaving[-1].start()
    for copy in leaving:
        copy.wait()


def pack(ids_row, queries, keys, values, per_step=4, folds=2):
    tokens = queries.shape[0]
    vmem = pl.BlockSpec(memory_space=pltpu.VMEM)
    hbm = pl.BlockSpec(memory_space=pltpu.HBM)
    outgoing, code = pl.pallas_call(
        pack_kernel,
        out_shape=(
            jax.ShapeDtypeStruct((folds, CTX // folds, CHUNK, HD), BF16),
            jax.ShapeDtypeStruct((1, tokens), jnp.int32),
        ),
        in_specs=[vmem, hbm, hbm, hbm],
        out_specs=(hbm, vmem),
        scratch_shapes=[
            pltpu.VMEM((3, tokens, HD), BF16),
            pltpu.VMEM((tokens, 3 * folds * HD), BF16),
            pltpu.VMEM((ROOM, tokens), BF16),
            pltpu.VMEM((per_step * ROOM, tokens), BF16),
            pltpu.VMEM((CTX, PAIR), F32),
            pltpu.VMEM((folds, CTX // folds, CHUNK, HD), BF16),
            pltpu.SemaphoreType.DMA((3,)),
            pltpu.SemaphoreType.DMA((folds, CTX // folds // per_step)),
        ],
        compiler_params=pltpu.CompilerParams(vmem_limit_bytes=60 << 20),
        cost_estimate=pl.CostEstimate(
            flops=2 * CTX * ROOM * tokens * 3 * HD, bytes_accessed=5 << 20, transcendentals=0
        ),
        name="pack",
    )(ids_row, queries, keys, values)
    return outgoing.reshape(CTX, CHUNK, HD), code


def mix_kernel(recv_ref, old_ref, out_ref, sums_ref, over_ref, wide, mixed, total):
    sources = recv_ref.shape[0]
    members = sources * SLOTS
    lanes = lax.broadcasted_iota(jnp.int32, (PAIR, HD), 1).astype(F32)
    index = lax.broadcasted_iota(jnp.int32, (ROOM, PAIR), 0).astype(F32)
    first_lane = (lax.broadcasted_iota(jnp.int32, (16, HD), 1) == 0).astype(BF16)
    ones = jnp.ones((members, HD), BF16)
    dims = (((1,), (1,)), ((), ()))

    flags = jnp.max(recv_ref[:, 3 * ROOM :, :].astype(F32), axis=0)
    over_ref[0, 0] = jnp.max(flags[1:2, :]).astype(jnp.int32)

    def slot_row(source):
        return recv_ref[source, 3 * ROOM :, :].astype(F32)[0:1, :]

    def expand(source):
        down = jnp.transpose(jnp.broadcast_to(slot_row(source), (PAIR, PAIR)))
        take = jnp.where(down == lanes, 1.0, 0.0).astype(BF16)[:, 0:ROOM]
        parts = [recv_ref[source, i * ROOM : (i + 1) * ROOM, :] for i in range(3)]
        found = jnp.dot(take, jnp.concatenate(parts, axis=1), preferred_element_type=F32)
        mark = jnp.where((down == NO_ROW) & (lanes == 0.0), EMPTY, 0.0)
        keys = found[:, HD : 2 * HD]
        total[...] += keys
        wide[0, :, source] = found[:, 0:HD].reshape(LOCAL, SLOTS, HD)
        wide[1, :, source] = (keys + mark).reshape(LOCAL, SLOTS, HD)
        wide[2, :, source] = found[:, 2 * HD :].reshape(LOCAL, SLOTS, HD)

    def attend_one(cluster):
        q, k, v = (wide[i, cluster].reshape(members, HD).astype(BF16) for i in range(3))
        both = jnp.concatenate([q, first_lane], axis=0)
        both = lax.dot_general(both, k, dims, preferred_element_type=F32)
        present = both[members : members + 1] < 0.5 * EMPTY
        scores = jnp.where(present, both[0:members], NEG_FILL)
        weights = jnp.exp2((scores - jnp.max(scores, axis=1, keepdims=True)) * EXP2_SCALE)
        totals = jnp.dot(
            weights.astype(BF16), jnp.concatenate([v, ones], axis=1), preferred_element_type=F32
        )
        mixed[:, cluster] = (totals[:, 0:HD] / totals[:, HD:]).reshape(sources, SLOTS, HD)

    def compress(source):
        put = jnp.where(index == slot_row(source), 1.0, 0.0).astype(BF16)
        slots = mixed[source].reshape(PAIR, HD).astype(BF16)
        out_ref[source] = jnp.dot(put, slots, preferred_element_type=F32).astype(BF16)

    def each(body, count, unroll):
        def some(step, carry):
            for i in range(unroll):
                body(step * unroll + i)
            return carry

        lax.fori_loop(0, count // unroll, some, 0)

    total[...] = jnp.zeros_like(total)
    each(expand, sources, sources)
    member_sums = jnp.sum(total[...].reshape(LOCAL, SLOTS, HD), axis=1)
    sums_ref[...] = DECAY * old_ref[...] + (1.0 - DECAY) * member_sums
    each(attend_one, LOCAL, LOCAL)
    each(compress, sources, sources)


def mix(recv, old_sums):
    return pl.pallas_call(
        mix_kernel,
        out_shape=(
            jax.ShapeDtypeStruct((CTX, ROOM, HD), BF16),
            jax.ShapeDtypeStruct((LOCAL, HD), F32),
            jax.ShapeDtypeStruct((1, 1), jnp.int32),
        ),
        in_specs=[pl.BlockSpec(memory_space=pltpu.VMEM)] * 2,
        out_specs=(
            pl.BlockSpec(memory_space=pltpu.VMEM),
            pl.BlockSpec(memory_space=pltpu.VMEM),
            pl.BlockSpec(memory_space=pltpu.SMEM),
        ),
        scratch_shapes=[
            pltpu.VMEM((3, LOCAL, CTX, SLOTS, HD), F32),
            pltpu.VMEM((CTX, LOCAL, SLOTS, HD), F32),
            pltpu.VMEM((PAIR, HD), F32),
        ],
        compiler_params=pltpu.CompilerParams(vmem_limit_bytes=32 << 20),
        cost_estimate=pl.CostEstimate(
            flops=4 * LOCAL * 256 * 256 * HD,
            bytes_accessed=5 << 20,
            transcendentals=LOCAL * 256 * 256,
        ),
        name="mix",
    )(recv, old_sums)


def unpack_kernel(code_ref, back_ref, out_ref, table):
    tokens = out_ref.shape[0]
    groups = table.shape[0] // PAIR

    @pl.when(pl.program_id(0) == 0)
    def _():
        for i in range(CTX):
            low, high = (i % groups) * PAIR, i // groups * HD
            table[low : low + ROOM, high : high + HD] = back_ref[i]
            table[low + ROOM : low + PAIR, high : high + HD] = jnp.zeros((PAIR - ROOM, HD), BF16)

    lanes = lax.broadcasted_iota(jnp.int32, (TILE, PAIR), 1)
    for j in range(tokens // TILE):
        here = code_ref[:, j * TILE : (j + 1) * TILE].astype(F32)
        down = jnp.transpose(jnp.broadcast_to(here, (TILE, TILE))).astype(jnp.int32)
        inner = down & (groups * PAIR - 1)
        outer = lax.shift_right_logical(down, (groups * PAIR).bit_length() - 1)
        hot = [jnp.where(inner == lanes + i * PAIR, 1.0, 0.0).astype(BF16) for i in range(groups)]
        found = jnp.dot(jnp.concatenate(hot, axis=1), table[...], preferred_element_type=F32)
        row = found[:, 0:HD]
        for i in range(1, CTX // groups):
            row = jnp.where(outer == i, found[:, i * HD : (i + 1) * HD], row)
        out_ref[j * TILE : (j + 1) * TILE, :] = row.astype(BF16)


def unpack(code, back, tile=2048, groups=8):
    tokens = code.shape[1]
    return pl.pallas_call(
        unpack_kernel,
        grid=(tokens // tile,),
        out_shape=jax.ShapeDtypeStruct((tokens, HD), BF16),
        in_specs=[
            pl.BlockSpec((1, tile), lambda s: (0, s)),
            pl.BlockSpec((CTX, ROOM, HD), lambda s: (0, 0, 0)),
        ],
        out_specs=pl.BlockSpec((tile, HD), lambda s: (s, 0)),
        scratch_shapes=[pltpu.VMEM((groups * PAIR, CTX // groups * HD), BF16)],
        compiler_params=pltpu.CompilerParams(
            dimension_semantics=("arbitrary",), vmem_limit_bytes=32 << 20
        ),
        cost_estimate=pl.CostEstimate(
            flops=2 * tokens * 1024 * 512, bytes_accessed=2 << 20, transcendentals=0
        ),
        name="unpack",
    )(code, back)


def hold_kernel(w_ref, out_ref, done):
    count = out_ref.shape[1]
    copies = [
        pltpu.make_async_copy(w_ref.at[c, pl.ds(0, count)], out_ref.at[c], done.at[c])
        for c in range(w_ref.shape[0])
    ]
    for copy in copies:
        copy.start()
    for copy in copies:
        copy.wait()


def hold(w_all, count=KEPT):
    halves, _, depth, width = w_all.shape
    return pl.pallas_call(
        hold_kernel,
        out_shape=jax.ShapeDtypeStruct((halves, count, depth, width), w_all.dtype),
        in_specs=[pl.BlockSpec(memory_space=pltpu.HBM)],
        out_specs=pl.BlockSpec(memory_space=pltpu.VMEM),
        scratch_shapes=[pltpu.SemaphoreType.DMA((halves,))],
        compiler_params=pltpu.CompilerParams(vmem_limit_bytes=8 << 20),
        cost_estimate=pl.CostEstimate(flops=0, bytes_accessed=16 << 20, transcendentals=0),
        name="hold",
    )(w_all)


def project_kernel(heads_ref, kept_ref, w_ref, out_ref, held, done):
    halves, steps, columns = held.shape[1], held.shape[0], held.shape[2]
    first = kept_ref.shape[1]
    each = heads_ref.shape[0] // halves
    copies = [
        [
            pltpu.make_async_copy(
                w_ref.at[c, pl.ds(first + p * columns, columns)], held.at[p, c], done.at[p, c]
            )
            for c in range(halves)
        ]
        for p in range(steps)
    ]
    for pair in copies:
        for copy in pair:
            copy.start()
    left = [
        jnp.concatenate([heads_ref[c * each + i] for i in range(each)], axis=1)
        for c in range(halves)
    ]

    def multiply(parts, low):
        total = 0.0
        for c, blocks in enumerate(parts):
            right = jnp.concatenate(blocks, axis=1)
            total = total + jnp.dot(left[c], right, preferred_element_type=F32)
        for n in range(len(parts[0])):
            out_ref[low + n] = total[:, n * HD : (n + 1) * HD].astype(BF16)

    multiply([[kept_ref[c, n] for n in range(first)] for c in range(halves)], 0)
    for p, pair in enumerate(copies):
        for copy in pair:
            copy.wait()
        multiply(
            [[held[p, c, n] for n in range(columns)] for c in range(halves)], first + p * columns
        )


def project(heads, kept, w_all, columns=4):
    halves, blocks, depth, width = w_all.shape
    tokens = heads.shape[1]
    steps = (blocks - kept.shape[1]) // columns
    vmem = pl.BlockSpec(memory_space=pltpu.VMEM)
    return pl.pallas_call(
        project_kernel,
        out_shape=jax.ShapeDtypeStruct((blocks, tokens, width), BF16),
        in_specs=[vmem, vmem, pl.BlockSpec(memory_space=pltpu.HBM)],
        out_specs=vmem,
        scratch_shapes=[
            pltpu.VMEM((steps, halves, columns, depth, width), BF16),
            pltpu.SemaphoreType.DMA((steps, halves)),
        ],
        compiler_params=pltpu.CompilerParams(vmem_limit_bytes=48 << 20),
        cost_estimate=pl.CostEstimate(
            flops=2 * tokens * halves * depth * blocks * width,
            bytes_accessed=9 << 20,
            transcendentals=0,
        ),
        name="project",
    )(heads, kept, w_all)


def over_ctx(chunks):
    return lax.all_to_all(chunks, "ctx", split_axis=0, concat_axis=0, tiled=True)


def on_device(queries, keys, values, cluster_ids, w_out, old_sums):
    hg_count = lax.axis_size("hg")
    tok_rows = queries.shape[0]
    half = w_out.shape[0] // 2
    w_half = lax.dynamic_slice_in_dim(w_out, lax.axis_index("ctx") % 2 * half, half)
    ids_row = cluster_ids[:, :, 0]
    outgoing, code = pack(ids_row, queries, keys, values)
    chips = [list(range(2 * hg_count * i, 2 * hg_count * (i + 1))) for i in range(CTX // 2)]
    w_all = lax.all_gather(w_half, ("ctx", "hg"), axis_index_groups=chips)
    mixed_rows, sums, over = mix(over_ctx(outgoing), old_sums[0])

    def compact():
        return unpack(code, over_ctx(mixed_rows)), sums

    def general():
        slots, target = place(ids_row, queries, keys, values)
        slot_rows, slot_sums = attend(over_ctx(slots), old_sums[0])
        return fetch(target, over_ctx(slot_rows)), slot_sums

    attention, centroid_sums = lax.switch(over[0, 0], [compact, general])
    attention = attention.reshape(hg_count, tok_rows // hg_count, HD)
    all_heads = lax.all_to_all(attention, "hg", split_axis=0, concat_axis=0, tiled=True)
    w_all = w_all.reshape(2, hg_count, -1, w_out.shape[1])
    mixed = project(all_heads, hold(w_all), w_all)
    projected = lax.all_to_all(mixed, "hg", split_axis=0, concat_axis=0, tiled=True)
    return (projected.reshape(tok_rows, w_out.shape[1]), centroid_sums[None])


def solution(mesh):
    placed = (
        P("ctx", "hg"),
        P("ctx", "hg"),
        P("ctx", "hg"),
        P("hg", "ctx", None),
        P(None, "hg"),
        P("hg", "ctx", None),
    )
    return jax.shard_map(
        on_device,
        mesh=mesh,
        in_specs=placed,
        out_specs=(P("ctx", "hg"), P("hg", "ctx", None)),
        check_vma=False,
    )
```
